32 devices in a mesh: seq: 4 (over x, core), fsdp: 8 (over z, y).
Axes of the slice: x: 2, y: 2, z: 4, core: 2. Of those that a mesh axis runs over, the one named last changes fastest.
Arguments:
- latent: bfloat16 [8, 1024, 1024], P('fsdp', 'seq'), may hold values from -6 to 6
- embed: bfloat16 [8, 1024, 1024], P('fsdp', 'seq'), may hold values from -6 to 6
- seg_ids: int32 [8, 1024], P('fsdp'), may hold values from 0 to 15, as said below
- positions: int32 [8, 1024], P('fsdp', 'seq'), may hold values from 0 to 511, as said below
- adapter_weight: bfloat16 [2048, 1024], P('fsdp'), may hold values from -0.125 to 0.125
- query_weight: bfloat16 [1024, 1024], P('fsdp'), may hold values from -0.1875 to 0.1875
- key_weight: bfloat16 [1024, 1024], P('fsdp'), may hold values from -0.1875 to 0.1875
- value_weight: bfloat16 [1024, 1024], P('fsdp'), may hold values from -0.1875 to 0.1875
- out_weight: bfloat16 [1024, 1024], P('fsdp'), may hold values from -1 to 1
- gate_weight: bfloat16 [1024, 2816], P('fsdp'), may hold values from -0.1875 to 0.1875
- up_weight: bfloat16 [1024, 2816], P('fsdp'), may hold values from -0.1875 to 0.1875
- down_weight: bfloat16 [2816, 1024], P('fsdp'), may hold values from -0.109375 to 0.109375
- gain_one: bfloat16 [1024], P('fsdp'), may hold values from 0.5 to 1.5
- gain_two: bfloat16 [1024], P('fsdp'), may hold values from 0.5 to 1.5
- gain_three: bfloat16 [1024], P('fsdp'), may hold values from 0.5 to 1.5
- gain_four: bfloat16 [1024], P('fsdp'), may hold values from 0.5 to 1.5
- cotangent: bfloat16 [8, 1024, 1024], P('fsdp', 'seq'), may hold values from -6 to 6
Outputs:
- output: bfloat16 [8, 1024, 1024], P('fsdp', 'seq')
- latent_grad: float32 [8, 1024, 1024], P('fsdp', 'seq')
- embed_grad: float32 [8, 1024, 1024], P('fsdp', 'seq')
- adapter_grad: float32 [2048, 1024], P('fsdp')
- query_grad: float32 [1024, 1024], P('fsdp')
- key_grad: float32 [1024, 1024], P('fsdp')
- value_grad: float32 [1024, 1024], P('fsdp')
- out_grad: float32 [1024, 1024], P('fsdp')
- gate_grad: float32 [1024, 2816], P('fsdp')
- up_grad: float32 [1024, 2816], P('fsdp')
- down_grad: float32 [2816, 1024], P('fsdp')
- gain_one_grad: float32 [1024], P('fsdp')
- gain_two_grad: float32 [1024], P('fsdp')
- gain_three_grad: float32 [1024], P('fsdp')
- gain_four_grad: float32 [1024], P('fsdp')
The draws below stay inside these ranges and needn't reach their ends.
Inputs may be any that keep to these rules, and one draw needn't show every extreme that they name: Each sequence packs exactly 16 documents: seg_ids start at 0, never fall and end at 15. Document lengths are heavy-tailed; one document of each sequence, at a place drawn from the seed, holds exactly 512 tokens. positions count the tokens from the start of each token's document (0 at each document's first token).
All inputs are finite; a program needn't handle non-finite values.
Results may differ from the reference program's by a relative error of at most 0.024.
Values may be sent and summed in bfloat16 or wider, within the bound.
No kernel may reach another device: no remote copies, remote signals or barrier semaphores. Data moves between devices by JAX's collectives and lax.ppermute only.
A program may use at most 192 MiB of HBM per device.

```python
import jax
import jax.numpy as jnp
from jax import lax

D = 1024
H = 16
HD = 64
FF = 2816
DOCS = 16
SEQ_LEN = 1024
SEQUENCES = 8


def document_layout(key):
    base_key = jax.random.fold_in(key, 11)
    first_key, second_key, third_key = jax.random.split(base_key, 3)
    others = DOCS - 1
    longest = SEQ_LEN // 2
    remaining = SEQ_LEN - longest
    factor = jax.random.randint(first_key, (SEQUENCES, others), 1, 5)
    power = jax.random.randint(second_key, (SEQUENCES, others), 0, 7)
    weights = (factor * jnp.power(2, power)).astype(jnp.int32)
    spare = remaining - others
    shares = spare * weights // jnp.sum(weights, axis=1, keepdims=True)
    shares = shares.astype(jnp.int32)
    leftover = spare - jnp.sum(shares, axis=1)
    shares = shares.at[:, others - 1].add(leftover)
    short_lengths = (shares + 1).astype(jnp.int32)
    place_long = jax.random.randint(third_key, (SEQUENCES, 1), 0, DOCS).astype(jnp.int32)
    index = jnp.arange(DOCS, dtype=jnp.int32)[None, :]
    source = jnp.clip(index - (index > place_long).astype(jnp.int32), 0, others - 1).astype(jnp.int32)
    picked = jnp.take_along_axis(short_lengths, source, axis=1)
    lengths = jnp.where(index == place_long, longest, picked).astype(jnp.int32)
    ends = jnp.cumsum(lengths, axis=1).astype(jnp.int32)
    begins = (ends - lengths).astype(jnp.int32)
    places = jnp.arange(SEQ_LEN, dtype=jnp.int32)
    segment = jnp.sum((places[None, :, None] >= ends[:, None, :]).astype(jnp.int32), axis=2)
    segment = jnp.minimum(segment, DOCS - 1).astype(jnp.int32)
    offset = jnp.take_along_axis(begins, segment, axis=1)
    return (segment, (places[None, :] - offset).astype(jnp.int32))


def draw_seg_ids(key, part):
    return document_layout(key)[0]


def draw_positions(key, part):
    return document_layout(key)[1]


def block_levels(own_key, dims, cuts, smallest, high):
    factor_of, own = 1.0, jax.random.fold_in(own_key, 6)
    for dim, parts in cuts:
        steps = jnp.exp(jax.random.uniform(jax.random.fold_in(own, dim), (parts,), jnp.float32, smallest / len(cuts), high / len(cuts)))
        factor_of = factor_of * jnp.repeat(steps, dims[dim] // parts).reshape([-1 if axis == dim else 1 for axis in range(len(dims))])
    return factor_of


def noise(stream_key, extent, width, bound, pieces=(), kind=jnp.bfloat16):
    drawn = width * jax.random.normal(stream_key, extent, jnp.float32)
    if pieces:
        drawn = drawn * block_levels(stream_key, extent, pieces, -0.22, 0.18)
    return jnp.clip(drawn, -bound, bound).astype(kind)


def setup_inputs(seed: int = 0) -> dict:
    keys = jax.random.split(jax.random.key(seed), 18)
    return {
        "latent": noise(keys[0], (SEQUENCES, SEQ_LEN, D), 1.0, 6.0, ((0, 8), (1, 4))),
        "embed": noise(keys[1], (SEQUENCES, SEQ_LEN, D), 1.0, 6.0, ((0, 8), (1, 4))),
        "seg_ids": draw_seg_ids(jax.random.fold_in(keys[17], 71), 0),
        "positions": draw_positions(jax.random.fold_in(keys[17], 71), 0),
        "adapter_weight": noise(keys[4], (2 * D, D), (2 * D) ** -0.5, 0.125, ((0, 8),)),
        "query_weight": noise(keys[5], (D, H * HD), D ** -0.5, 0.1875, ((0, 8),)),
        "key_weight": noise(keys[6], (D, H * HD), D ** -0.5, 0.1875, ((0, 8),)),
        "value_weight": noise(keys[7], (D, H * HD), D ** -0.5, 0.1875, ((0, 8),)),
        "out_weight": noise(keys[8], (H * HD, D), (H * HD // 32) ** -0.5, 1.0, ((0, 8),)),
        "gate_weight": noise(keys[9], (D, FF), D ** -0.5, 0.1875, ((0, 8),)),
        "up_weight": noise(keys[10], (D, FF), D ** -0.5, 0.1875, ((0, 8),)),
        "down_weight": noise(keys[11], (FF, D), FF ** -0.5, 0.109375, ((0, 8),)),
        "gain_one": jnp.clip(1.0 + 0.1 * jax.random.normal(keys[12], (D,), jnp.float32), 0.5, 1.5).astype(jnp.bfloat16),
        "gain_two": jnp.clip(1.0 + 0.1 * jax.random.normal(keys[13], (D,), jnp.float32), 0.5, 1.5).astype(jnp.bfloat16),
        "gain_three": jnp.clip(1.0 + 0.1 * jax.random.normal(keys[14], (D,), jnp.float32), 0.5, 1.5).astype(jnp.bfloat16),
        "gain_four": jnp.clip(1.0 + 0.1 * jax.random.normal(keys[15], (D,), jnp.float32), 0.5, 1.5).astype(jnp.bfloat16),
        "cotangent": noise(keys[16], (SEQUENCES, SEQ_LEN, D), 1.0, 6.0, ((0, 8), (1, 4))),
    }


EPSILON = 1e-06
ROPE_BASE = 50000.0
NEG_FILL = -1e+30

@jax.custom_vjp
def low(v):
    return lax.optimization_barrier(v.astype(jnp.bfloat16)).astype(jnp.float32)

@jax.custom_vjp
def low_back(v):
    return v

def low_keep(v):
    return (low(v), None)

def low_pass(kept, grad):
    return (grad,)

def back_keep(v):
    return (v, None)

def back_low(kept, grad):
    return (low(grad),)
low.defvjp(low_keep, low_pass)
low_back.defvjp(back_keep, back_low)

def matmul_high(left, right):
    return jnp.dot(left, right, precision=lax.Precision.HIGHEST, preferred_element_type=jnp.float32)

def rms_norm(values):
    return values * lax.rsqrt(lax.optimization_barrier(jnp.mean(values * values, axis=-1, keepdims=True)) + EPSILON)

def rotate(values, places):
    half_width = values.shape[-1] // 2
    frequency = ROPE_BASE ** (-2.0 * jnp.arange(half_width, dtype=jnp.float32) / values.shape[-1])
    angles = places.astype(jnp.float32)[:, None] * frequency[None, :]
    cosine_table = jnp.cos(angles)[:, None, :]
    sine_table = jnp.sin(angles)[:, None, :]
    leading = values[..., :half_width]
    trailing = values[..., half_width:]
    return jnp.concatenate([leading * cosine_table - trailing * sine_table, trailing * cosine_table + leading * sine_table], axis=-1)

def attend(query_rows, key_rows, value_rows, segments):
    length = query_rows.shape[0]
    block_rows = min(512, length)
    factor = HD ** (-0.5)
    key_index = jnp.arange(length, dtype=jnp.int32)

    def one_block(begin):
        query_block = lax.dynamic_slice_in_dim(query_rows, begin, block_rows, 0)
        query_segs = lax.dynamic_slice_in_dim(segments, begin, block_rows, 0)
        query_index = begin + jnp.arange(block_rows, dtype=jnp.int32)
        scores = jnp.einsum('qhd,khd->hqk', query_block, key_rows, precision=lax.Precision.HIGHEST) * factor
        scores = low_back(scores)
        allowed = (query_segs[:, None] == segments[None, :]) & (key_index[None, :] <= query_index[:, None])
        scores = jnp.where(allowed[None], scores, NEG_FILL)
        highest = lax.optimization_barrier(jnp.max(scores, axis=-1, keepdims=True))
        expos = jnp.exp(scores - highest)
        probs = expos / lax.optimization_barrier(jnp.sum(expos, axis=-1, keepdims=True))
        return jnp.einsum('hqk,khd->qhd', low(probs), value_rows, precision=lax.Precision.HIGHEST)
    begins = (jnp.arange(length // block_rows) * block_rows).astype(jnp.int32)
    result = lax.map(jax.checkpoint(one_block), begins)
    return result.reshape(length, query_rows.shape[1], query_rows.shape[2])

def block_layer(joined, weights, segments, places):
    adapter_w, query_w, key_w, value_w, out_w, gate_w, up_w, down_w, gain_a, gain_b, gain_c, gain_d = weights
    length = joined.shape[0]
    stream = low_back(matmul_high(joined, adapter_w))
    normed_one = low(rms_norm(stream) * gain_a)
    query_lin = low_back(matmul_high(normed_one, query_w)).reshape(length, H, HD)
    key_lin = low_back(matmul_high(normed_one, key_w)).reshape(length, H, HD)
    value_rows = low(low_back(matmul_high(normed_one, value_w))).reshape(length, H, HD)
    query_rows = low(low_back(rotate(query_lin, places)))
    key_rows = low(low_back(rotate(key_lin, places)))
    attended = low(low_back(attend(query_rows, key_rows, value_rows, segments))).reshape(length, H * HD)
    branch = low_back(matmul_high(attended, out_w))
    middle = rms_norm(branch + stream) * gain_b
    normed_three = low(rms_norm(middle) * gain_c)
    gate = low_back(matmul_high(normed_three, gate_w))
    upper = low_back(matmul_high(normed_three, up_w))
    hidden = low(gate / (1.0 + jnp.exp(-gate)) * upper)
    mlp_out = low_back(matmul_high(hidden, down_w))
    return rms_norm(mlp_out + middle) * gain_d

def reference(latent, embed, seg_ids, positions, adapter_weight, query_weight, key_weight, value_weight, out_weight, gate_weight, up_weight, down_weight, gain_one, gain_two, gain_three, gain_four, cotangent):
    weights = tuple((item.astype(jnp.float32) for item in (adapter_weight, query_weight, key_weight, value_weight, out_weight, gate_weight, up_weight, down_weight, gain_one, gain_two, gain_three, gain_four)))

    def per_sequence(totals, sequence_item):
        latent_row, embed_row, segments, places, upstream = sequence_item
        joined = jnp.concatenate([latent_row, embed_row], axis=-1).astype(jnp.float32)

        def forward(joined_in, weights_in):
            return block_layer(joined_in, weights_in, segments, places)
        result, pull = jax.vjp(forward, joined, weights)
        joined_grad, weight_grads = pull(upstream.astype(jnp.float32))
        totals = tuple((running + extra for running, extra in zip(totals, weight_grads)))
        return (totals, (result.astype(jnp.bfloat16), joined_grad))
    initial = tuple((jnp.zeros(item.shape, jnp.float32) for item in weights))
    totals, (outputs, joined_grads) = lax.scan(per_sequence, initial, (latent, embed, seg_ids, positions, cotangent))
    return (outputs, joined_grads[..., :D], joined_grads[..., D:], totals[0], totals[1], totals[2], totals[3], totals[4], totals[5], totals[6], totals[7], totals[8], totals[9], totals[10], totals[11])
```

```python
import jax
import jax.numpy as jnp
import numpy as np
from jax import lax
from jax.experimental import pallas as pl
from jax.experimental.pallas import tpu as pltpu
from jax.sharding import PartitionSpec as P

H = 16
HD = 64
EPSILON = 1e-06
ROPE_BASE = 50000.0
NEG_FILL = -1e30
BLOCK = 256
F32 = jnp.float32
BF16 = jnp.bfloat16


def dot_nn(left, right):
    return lax.dot_general(left, right, (((1,), (0,)), ((), ())), preferred_element_type=F32)


def dot_tn(left, right):
    return lax.dot_general(left, right, (((0,), (0,)), ((), ())), preferred_element_type=F32)


def dot_nt(left, right):
    return lax.dot_general(left, right, (((1,), (1,)), ((), ())), preferred_element_type=F32)


def inverse_root(values):
    return lax.rsqrt(jnp.mean(values * values, axis=-1, keepdims=True) + EPSILON)


def norm_back(values, root, upstream):
    inner_mean = jnp.mean(upstream * values, axis=-1, keepdims=True)
    return root * upstream - values * root * root * root * inner_mean


def swap_halves(values):
    lane = lax.broadcasted_iota(jnp.int32, values.shape, 1)
    width = values.shape[1]
    ahead = pltpu.roll(values, width - HD // 2, 1)
    behind = pltpu.roll(values, HD // 2, 1)
    return jnp.where(lane % HD < HD // 2, ahead, behind)


def stack_heads(rows):
    lane = lax.broadcasted_iota(jnp.int32, rows.shape, 1)
    zero = jnp.zeros_like(rows)
    count = rows.shape[1] // HD
    return jnp.concatenate([jnp.where(lane // HD == h, rows, zero) for h in range(count)], axis=0)


def allowed_block(key_segs, query_segs, key_begin, query_begin, count):
    rows, cols = key_segs.shape[0], query_segs.shape[1]
    key_index = key_begin + lax.broadcasted_iota(jnp.int32, (rows, cols), 0)
    query_index = query_begin + lax.broadcasted_iota(jnp.int32, (rows, cols), 1)
    keep = (key_segs == query_segs) & (key_index <= query_index)
    bias = jnp.where(keep, 0.0, NEG_FILL)
    return jnp.concatenate([bias] * count, axis=1)


def forward_kernel(
    first_ref,
    q_ref,
    k_ref,
    v_ref,
    cosq_ref,
    sinq_ref,
    cosk_ref,
    sink_ref,
    segq_ref,
    segk_ref,
    out_ref,
    qrow_ref,
    krow_ref,
    vrow_ref,
    lse_ref,
    score_ref,
    acc_ref,
):
    i = pl.program_id(0)
    heads = q_ref.shape[1] // HD

    @pl.when(i == 0)
    def _():
        keys = k_ref[...]
        krow_ref[...] = (keys * cosk_ref[...] + swap_halves(keys) * sink_ref[...]).astype(BF16)
        vrow_ref[...] = v_ref[...].astype(BF16)

    queries = q_ref[...]
    rows = (queries * cosq_ref[...] + swap_halves(queries) * sinq_ref[...]).astype(BF16)
    qrow_ref[...] = rows
    stacked = stack_heads(rows * jnp.asarray(HD ** (-0.5), BF16))
    begin = first_ref[i]
    wide = heads * BLOCK

    def score_step(j, high):
        base = pl.multiple_of(j * BLOCK, BLOCK)
        keys = krow_ref[pl.ds(base, BLOCK), :]
        scores = dot_nt(keys, stacked)
        scores = scores + allowed_block(
            segk_ref[pl.ds(base, BLOCK), :1], segq_ref[0], base, i * BLOCK, heads
        )
        score_ref[pl.ds(base, BLOCK), :] = scores
        return jnp.maximum(high, jnp.max(scores, axis=0, keepdims=True))

    high = lax.fori_loop(begin, i + 1, score_step, jnp.full((1, wide), NEG_FILL, F32))
    acc_ref[...] = jnp.zeros_like(acc_ref)

    def value_step(j, total):
        base = pl.multiple_of(j * BLOCK, BLOCK)
        expos = jnp.exp(score_ref[pl.ds(base, BLOCK), :] - high)
        values = vrow_ref[pl.ds(base, BLOCK), :]
        acc_ref[...] += dot_tn(values, expos.astype(BF16))
        return total + jnp.sum(expos, axis=0, keepdims=True)

    total = lax.fori_loop(begin, i + 1, value_step, jnp.zeros((1, wide), F32))
    scaled = acc_ref[...] / total
    pieces = [
        scaled[h * HD : (h + 1) * HD, h * BLOCK : (h + 1) * BLOCK] for h in range(heads)
    ]
    out_ref[...] = jnp.transpose(jnp.concatenate(pieces, axis=0), (1, 0)).astype(BF16)
    lse_ref[0] = high + jnp.log(total)


def attend_forward(qkv, cosine, sine, seg_row, seg_col, first):
    length = qkv.shape[0]
    width = qkv.shape[1] // 3
    heads = width // HD
    blocks = length // BLOCK
    part = pl.BlockSpec((BLOCK, width), lambda i, first: (i, 0))
    whole = pl.BlockSpec((length, width), lambda i, first: (0, 0))
    return pl.pallas_call(
        forward_kernel,
        grid_spec=pltpu.PrefetchScalarGridSpec(
            num_scalar_prefetch=1,
            grid=(blocks,),
            in_specs=[
                part,
                pl.BlockSpec((length, width), lambda i, first: (0, 1)),
                pl.BlockSpec((length, width), lambda i, first: (0, 2)),
                part,
                part,
                whole,
                whole,
                pl.BlockSpec((1, 1, BLOCK), lambda i, first: (i, 0, 0)),
                pl.BlockSpec((length, 128), lambda i, first: (0, 0)),
            ],
            out_specs=[
                part,
                part,
                whole,
                whole,
                pl.BlockSpec((1, 1, heads * BLOCK), lambda i, first: (i, 0, 0)),
            ],
            scratch_shapes=[
                pltpu.VMEM((length, heads * BLOCK), F32),
                pltpu.VMEM((width, heads * BLOCK), F32),
            ],
        ),
        out_shape=[
            jax.ShapeDtypeStruct((length, width), BF16),
            jax.ShapeDtypeStruct((length, width), BF16),
            jax.ShapeDtypeStruct((length, width), BF16),
            jax.ShapeDtypeStruct((length, width), BF16),
            jax.ShapeDtypeStruct((blocks, 1, heads * BLOCK), F32),
        ],
        cost_estimate=pl.CostEstimate(
            flops=4 * length * length * width, bytes_accessed=8 << 20, transcendentals=0
        ),
        name="attend_forward",
    )(first, qkv, qkv, qkv, cosine, sine, cosine, sine, seg_row, seg_col)


def backward_kernel(
    first_ref,
    q_ref,
    k_ref,
    v_ref,
    grad_ref,
    out_ref,
    lse_ref,
    cosq_ref,
    sinq_ref,
    cosk_ref,
    sink_ref,
    segq_ref,
    segk_ref,
    dq_ref,
    dk_ref,
    dv_ref,
    dk_acc,
    dv_acc,
    dq_acc,
):
    i = pl.program_id(0)
    heads = q_ref.shape[1] // HD
    factor = HD ** (-0.5)

    @pl.when(i == 0)
    def _():
        dk_acc[...] = jnp.zeros_like(dk_acc)
        dv_acc[...] = jnp.zeros_like(dv_acc)

    stacked = stack_heads(q_ref[...] * jnp.asarray(factor, BF16))
    grads = grad_ref[...]
    grad_stacked = stack_heads(grads)
    product = jnp.transpose(grads.astype(F32) * out_ref[...].astype(F32), (1, 0))
    inner = jnp.concatenate(
        [
            jnp.sum(product[h * HD : (h + 1) * HD, :], axis=0, keepdims=True)
            for h in range(heads)
        ],
        axis=1,
    )
    log_sum = lse_ref[0]
    dq_acc[...] = jnp.zeros_like(dq_acc)

    def step(j, carry):
        base = pl.multiple_of(j * BLOCK, BLOCK)
        keys = k_ref[pl.ds(base, BLOCK), :]
        values = v_ref[pl.ds(base, BLOCK), :]
        scores = dot_nt(keys, stacked)
        scores = scores + allowed_block(
            segk_ref[pl.ds(base, BLOCK), :1], segq_ref[0], base, i * BLOCK, heads
        )
        probs = jnp.exp(scores - log_sum)
        dv_acc[pl.ds(base, BLOCK), :] += dot_nn(probs.astype(BF16), grad_stacked)
        grad_probs = dot_nt(values, grad_stacked)
        grad_scores = (probs * (grad_probs - inner)).astype(BF16)
        dk_acc[pl.ds(base, BLOCK), :] += dot_nn(grad_scores, stacked)
        dq_acc[...] += dot_tn(keys, grad_scores)
        return carry

    lax.fori_loop(first_ref[i], i + 1, step, 0)
    pieces = [
        dq_acc[h * HD : (h + 1) * HD, h * BLOCK : (h + 1) * BLOCK] for h in range(heads)
    ]
    dq = jnp.transpose(jnp.concatenate(pieces, axis=0), (1, 0)) * factor
    dq = dq.astype(BF16).astype(F32)
    dq_ref[...] = (dq * cosq_ref[...] - swap_halves(dq) * sinq_ref[...]).astype(BF16)

    @pl.when(i == pl.num_programs(0) - 1)
    def _():
        dk = dk_acc[...].astype(BF16).astype(F32)
        dk_ref[...] = (dk * cosk_ref[...] - swap_halves(dk) * sink_ref[...]).astype(BF16)
        dv_ref[...] = dv_acc[...].astype(BF16)


def attend_backward(q_rows, k_rows, v_rows, grads, outs, lse, cosine, sine, seg_row, seg_col, first):
    length, width = q_rows.shape
    heads = width // HD
    blocks = length // BLOCK
    part = pl.BlockSpec((BLOCK, width), lambda i, first: (i, 0))
    whole = pl.BlockSpec((length, width), lambda i, first: (0, 0))
    return pl.pallas_call(
        backward_kernel,
        grid_spec=pltpu.PrefetchScalarGridSpec(
            num_scalar_prefetch=1,
            grid=(blocks,),
            in_specs=[
                part,
                whole,
                whole,
                part,
                part,
                pl.BlockSpec((1, 1, heads * BLOCK), lambda i, first: (i, 0, 0)),
                part,
                part,
                whole,
                whole,
                pl.BlockSpec((1, 1, BLOCK), lambda i, first: (i, 0, 0)),
                pl.BlockSpec((length, 128), lambda i, first: (0, 0)),
            ],
            out_specs=[part, whole, whole],
            scratch_shapes=[
                pltpu.VMEM((length, width), F32),
                pltpu.VMEM((length, width), F32),
                pltpu.VMEM((width, heads * BLOCK), F32),
            ],
        ),
        out_shape=[jax.ShapeDtypeStruct((length, width), BF16) for _ in range(3)],
        cost_estimate=pl.CostEstimate(
            flops=10 * length * length * width, bytes_accessed=10 << 20, transcendentals=0
        ),
        name="attend_backward",
    )(
        first,
        q_rows,
        k_rows,
        v_rows,
        grads,
        outs,
        lse,
        cosine,
        sine,
        cosine,
        sine,
        seg_row,
        seg_col,
    )


def flip(array, bits, count=4):
    return lax.ppermute(array, "seq", [(i, i ^ bits) for i in range(count)])


def place(pieces, member):
    stacked = jnp.zeros((len(pieces),) + pieces[0].shape, pieces[0].dtype)
    for k, piece in enumerate(pieces):
        stacked = lax.dynamic_update_index_in_dim(stacked, piece, member ^ k, 0)
    return stacked


def gather_seq(own, member):
    across = flip(own, 2)
    beside = flip(own, 1)
    return place([own, beside, across, flip(across, 1)], member)


def scatter_seq(partial, member):
    blocks = partial.reshape(4, partial.shape[0] // 4, partial.shape[1])

    def block(k):
        return lax.dynamic_index_in_dim(blocks, member ^ k, 0, keepdims=False)

    far = flip(block(3).astype(BF16), 1)
    near = flip(block(1).astype(BF16), 1)
    crossing = flip((block(2) + far.astype(F32)).astype(BF16), 2)
    return block(0) + near.astype(F32) + crossing.astype(F32)


def swap_seq(blocks, member):
    pieces = [lax.dynamic_index_in_dim(blocks, member, 0, keepdims=False)]
    for k in (1, 2, 3):
        piece = lax.dynamic_index_in_dim(blocks, member ^ k, 0, keepdims=False)
        pieces.append(flip(piece, k))
    return place(pieces, member)


class Ring:
    def __init__(self, count):
        order = list(range(count))
        if count == 8:
            order = [0, 2, 4, 6, 7, 5, 3, 1]
        self.count = count
        self.order = np.array(order, np.int32)
        inverse = np.argsort(self.order).astype(np.int32)
        self.at = jnp.asarray(inverse)[lax.axis_index("fsdp")]
        nxt = [(order[i], order[(i + 1) % count]) for i in range(count)]
        self.perm = {1: nxt, -1: [(b, a) for a, b in nxt]}

    def send(self, array, way):
        return lax.ppermute(array, "fsdp", self.perm[way])

    def shard(self, offset):
        return jnp.asarray(self.order)[(self.at + offset) % self.count]

    def gather(self, own):
        rows = own.shape[0]
        half = (rows // 2 + 7) // 8 * 8
        full = jnp.zeros((self.count,) + own.shape, own.dtype)

        def put(full, piece, offset, row=0):
            return lax.dynamic_update_slice(full, piece[None], (self.shard(offset), row, 0))

        full = put(full, own, 0)
        ahead = behind = own
        for t in range(1, self.count // 2):
            ahead, behind = self.send(ahead, 1), self.send(behind, -1)
            full = put(put(full, ahead, -t), behind, t)
        last = self.count // 2
        full = put(full, self.send(ahead[:half], 1), -last)
        return put(full, self.send(behind[half:], -1), last, half)

    def scatter(self, parts):
        rows = parts.shape[1]
        half = (rows // 2 + 7) // 8 * 8

        def local(offset):
            return lax.dynamic_index_in_dim(parts, self.shard(offset), 0, keepdims=False)

        last = self.count // 2
        far = local(last)
        ahead = self.send(far[:half], 1)
        behind = self.send(far[half:], -1)
        for t in range(last - 1, 0, -1):
            front, back = local(t), local(-t)
            if t == last - 1:
                front = jnp.concatenate([add(front[:half], ahead), front[half:]], axis=0)
                back = jnp.concatenate([back[:half], add(back[half:], behind)], axis=0)
            else:
                front, back = add(front, ahead), add(back, behind)
            ahead, behind = self.send(front, 1), self.send(back, -1)
        return local(0).astype(F32) + ahead.astype(F32) + behind.astype(F32)


def add(left, right):
    return (left.astype(F32) + right.astype(F32)).astype(BF16)


def per_device(
    latent,
    embed,
    seg_ids,
    positions,
    adapter_weight,
    query_weight,
    key_weight,
    value_weight,
    out_weight,
    gate_weight,
    up_weight,
    down_weight,
    gain_one,
    gain_two,
    gain_three,
    gain_four,
    cotangent,
):
    member = lax.axis_index("seq")
    count = lax.axis_size("fsdp")
    ring = Ring(count)
    tokens, width = latent.shape[1], latent.shape[2]
    length = tokens * 4
    quarter = width // 4
    rows = query_weight.shape[0]
    hidden_rows = down_weight.shape[0] // 4
    hidden_width = hidden_rows * count

    def columns(weight):
        return lax.dynamic_slice_in_dim(weight, member * quarter, quarter, 1)

    def hidden_columns(weight):
        split = weight.reshape(rows, count, 4, hidden_rows)
        return lax.dynamic_index_in_dim(split, member, 2, keepdims=False).reshape(
            rows, hidden_width
        )

    joined = jnp.concatenate([latent[0], embed[0]], axis=1)
    gains = jnp.concatenate([gain_one, gain_two, gain_three, gain_four])
    gain_rows = -(-gains.shape[0] // (8 * quarter)) * 8
    gains = jnp.pad(gains, (0, gain_rows * quarter - gains.shape[0])).reshape(gain_rows, quarter)
    adapter_rows = adapter_weight.shape[0]

    joined_all = gather_seq(joined, member).reshape(length, 2 * width)
    first_group = ring.gather(jnp.concatenate([columns(adapter_weight), gains], axis=0))
    adapter_cols = first_group[:, :adapter_rows].reshape(2 * width, quarter)
    gains_all = first_group[:, adapter_rows:].reshape(count, gain_rows * quarter)
    gains_all = gains_all[:, : 4 * rows].reshape(count, 4, rows)
    gain_a, gain_b, gain_c, gain_d = [
        gains_all[:, g].reshape(1, width).astype(F32) for g in range(4)
    ]
    qkvo = ring.gather(
        jnp.concatenate(
            [columns(query_weight), columns(key_weight), columns(value_weight), columns(out_weight)],
            axis=1,
        )
    ).reshape(width, width)
    qkv_cols = qkvo[:, : 3 * quarter]
    out_blocks = swap_seq(qkvo[:, 3 * quarter :].reshape(4, quarter, quarter), member)
    out_rows = jnp.concatenate([out_blocks[m] for m in range(4)], axis=1)
    gate_up = ring.gather(
        jnp.concatenate([hidden_columns(gate_weight), hidden_columns(up_weight)], axis=1)
    ).reshape(width, 2 * hidden_width)
    down_rows = ring.gather(
        lax.dynamic_slice_in_dim(down_weight, member * hidden_rows, hidden_rows, 0)
    ).reshape(hidden_width, width)

    segments = seg_ids[0]
    starts = jnp.sum((segments[None, :] < segments[:, None]).astype(jnp.int32), axis=1)
    places = (jnp.arange(length, dtype=jnp.int32) - starts).astype(F32)
    first = starts[::BLOCK] // BLOCK
    half = HD // 2
    frequency = ROPE_BASE ** (-2.0 * jnp.arange(half, dtype=F32) / HD)
    angles = places[:, None] * frequency[None, :]
    cos_half, sin_half = jnp.cos(angles), jnp.sin(angles)
    cosine = jnp.tile(cos_half, (1, 2 * quarter // HD))
    sine = jnp.tile(jnp.concatenate([-sin_half, sin_half], axis=1), (1, quarter // HD))
    seg_row = segments.reshape(length // BLOCK, 1, BLOCK)
    seg_col = jnp.broadcast_to(segments[:, None], (length, 128))

    stream_cols = dot_nn(joined_all, adapter_cols).astype(BF16)
    stream_blocks = gather_seq(stream_cols, member)
    stream_all = jnp.concatenate([stream_blocks[m] for m in range(4)], axis=1).astype(F32)
    normed_one = (stream_all * inverse_root(stream_all) * gain_a).astype(BF16)
    stream = lax.dynamic_slice_in_dim(stream_blocks, member * tokens, tokens, 1)
    stream = jnp.concatenate([stream[m] for m in range(4)], axis=1).astype(F32)
    root_one = inverse_root(stream)
    qkv = dot_nn(normed_one, qkv_cols)
    attended, q_rows, k_rows, v_rows, lse = attend_forward(
        qkv, cosine, sine, seg_row, seg_col, first
    )
    resid_one = scatter_seq(dot_nn(attended, out_rows), member) + stream
    root_two = inverse_root(resid_one)
    middle = resid_one * root_two * gain_b
    root_three = inverse_root(middle)
    normed_three = (middle * root_three * gain_c).astype(BF16)
    normed_three = gather_seq(normed_three, member).reshape(length, width)
    gate_up_act = dot_nn(normed_three, gate_up)
    gate_act, up_act = gate_up_act[:, :hidden_width], gate_up_act[:, hidden_width:]
    sigmoid_gate = 1.0 / (1.0 + jnp.exp(-gate_act))
    silu_gate = gate_act * sigmoid_gate
    hidden = (silu_gate * up_act).astype(BF16)
    resid_two = scatter_seq(dot_nn(hidden, down_rows), member) + middle
    root_four = inverse_root(resid_two)
    result = (resid_two * root_four * gain_d).astype(BF16)

    upstream = cotangent[0].astype(F32)
    gain_four_part = jnp.sum(upstream * resid_two * root_four, axis=0)
    d_resid_two = norm_back(resid_two, root_four, upstream * gain_d)
    d_mlp = gather_seq(d_resid_two.astype(BF16), member).reshape(length, width)
    down_part = dot_tn(hidden, d_mlp).astype(BF16)
    d_hidden = dot_nt(d_mlp, down_rows)
    d_gate = (d_hidden * up_act * sigmoid_gate * (1.0 + gate_act * (1.0 - sigmoid_gate))).astype(
        BF16
    )
    d_up = (d_hidden * silu_gate).astype(BF16)
    d_gate_up = jnp.concatenate([d_gate, d_up], axis=1)
    gate_up_part = dot_tn(normed_three, d_gate_up).astype(BF16)
    d_normed_three = scatter_seq(dot_nt(d_gate_up, gate_up), member)
    gain_three_part = jnp.sum(d_normed_three * middle * root_three, axis=0)
    d_middle = d_resid_two + norm_back(middle, root_three, d_normed_three * gain_c)
    gain_two_part = jnp.sum(d_middle * resid_one * root_two, axis=0)
    d_resid_one = norm_back(resid_one, root_two, d_middle * gain_b)
    d_branch = gather_seq(d_resid_one.astype(BF16), member).reshape(length, width)
    out_part = dot_tn(attended, d_branch).astype(BF16)
    d_attended = dot_nt(d_branch, out_rows).astype(BF16)
    dq, dk, dv = attend_backward(
        q_rows, k_rows, v_rows, d_attended, attended, lse, cosine, sine, seg_row, seg_col, first
    )
    d_qkv = jnp.concatenate([dq, dk, dv], axis=1)
    qkv_part = dot_tn(normed_one, d_qkv).astype(BF16)
    d_normed_one = scatter_seq(dot_nt(d_qkv, qkv_cols), member)
    gain_one_part = jnp.sum(d_normed_one * stream * root_one, axis=0)
    d_stream = (d_resid_one + norm_back(stream, root_one, d_normed_one * gain_a)).astype(BF16)
    adapter_blocks = gather_seq(adapter_cols, member)
    d_joined = sum(
        dot_nt(d_stream[:, m * quarter : (m + 1) * quarter], adapter_blocks[m]) for m in range(4)
    )
    d_stream_blocks = jnp.stack(
        [d_stream[:, m * quarter : (m + 1) * quarter] for m in range(4)], axis=0
    )
    d_stream_cols = swap_seq(d_stream_blocks, member).reshape(length, quarter)
    adapter_part = dot_tn(joined_all, d_stream_cols).astype(BF16)

    def shares(part):
        return part.reshape(count, part.shape[0] // count, part.shape[1])

    def finish(total):
        return gather_seq(total.astype(BF16), member)

    down_done = finish(ring.scatter(shares(down_part)))
    down_grad = down_done.astype(F32).reshape(4 * hidden_rows, width)
    gate_up_done = finish(ring.scatter(shares(gate_up_part)))
    gate_up_done = gate_up_done.reshape(4, rows, 2, count, hidden_rows).astype(F32)
    gate_up_done = jnp.transpose(gate_up_done, (2, 1, 3, 0, 4)).reshape(2, rows, 4 * hidden_width)
    gate_grad, up_grad = gate_up_done[0], gate_up_done[1]
    out_part = jnp.stack(
        [out_part[:, m * quarter : (m + 1) * quarter] for m in range(4)], axis=0
    )
    out_part = swap_seq(out_part, member).reshape(width, quarter)
    out_done = finish(ring.scatter(shares(out_part)))
    qkv_done = finish(ring.scatter(shares(qkv_part)))
    gain_parts = jnp.stack([gain_one_part, gain_two_part, gain_three_part, gain_four_part])
    gain_parts = jnp.transpose(gain_parts.reshape(4, count, rows), (1, 0, 2))
    gain_parts = jnp.pad(
        gain_parts.reshape(count, 4 * rows), ((0, 0), (0, gain_rows * quarter - 4 * rows))
    ).reshape(count, gain_rows, quarter)
    last_done = finish(
        ring.scatter(jnp.concatenate([shares(adapter_part), gain_parts.astype(BF16)], axis=1))
    )

    def wide(done, low, high):
        return jnp.concatenate([done[m, :, low:high] for m in range(4)], axis=1).astype(F32)

    adapter_grad = wide(last_done[:, :adapter_rows], 0, quarter)
    gain_sums = jnp.sum(last_done[:, adapter_rows:].astype(F32), axis=0)
    gain_sums = gain_sums.reshape(gain_rows * quarter)[: 4 * rows].reshape(4, rows)
    return (
        result[None],
        d_joined[:, :width][None],
        d_joined[:, width:][None],
        adapter_grad,
        wide(qkv_done, 0, quarter),
        wide(qkv_done, quarter, 2 * quarter),
        wide(qkv_done, 2 * quarter, 3 * quarter),
        wide(out_done, 0, quarter),
        gate_grad,
        up_grad,
        down_grad,
        gain_sums[0],
        gain_sums[1],
        gain_sums[2],
        gain_sums[3],
    )


def solution(mesh):
    rows, vector = P("fsdp", None), P("fsdp")
    tokens = P("fsdp", "seq", None)
    placed = (tokens, tokens, rows, P("fsdp", "seq")) + (rows,) * 8 + (vector,) * 4 + (tokens,)
    return jax.shard_map(
        per_device,
        mesh=mesh,
        in_specs=placed,
        out_specs=(tokens,) * 3 + (rows,) * 8 + (vector,) * 4,
        check_vma=False,
    )
```

```python
import jax
import jax.numpy as jnp
import numpy as np
from jax import lax
from jax.experimental import pallas as pl
from jax.experimental.pallas import tpu as pltpu
from jax.sharding import PartitionSpec as P

H = 16
HD = 64
EPSILON = 1e-06
ROPE_BASE = 50000.0
NEG_FILL = -1e30
BLOCK = 256
F32 = jnp.float32
SMALL = pl.CostEstimate(flops=1, bytes_accessed=1, transcendentals=0)
BF16 = jnp.bfloat16


def dot_nn(left, right):
    return lax.dot_general(left, right, (((1,), (0,)), ((), ())), preferred_element_type=F32)


def dot_tn(left, right):
    return lax.dot_general(left, right, (((0,), (0,)), ((), ())), preferred_element_type=F32)


def dot_nt(left, right):
    return lax.dot_general(left, right, (((1,), (1,)), ((), ())), preferred_element_type=F32)


def inverse_root(values):
    return lax.rsqrt(jnp.mean(values * values, axis=-1, keepdims=True) + EPSILON)


def norm_back(values, root, upstream):
    inner_mean = jnp.mean(upstream * values, axis=-1, keepdims=True)
    return root * upstream - values * root * root * root * inner_mean


def swap_halves(values):
    lane = lax.broadcasted_iota(jnp.int32, values.shape, 1)
    width = values.shape[1]
    ahead = pltpu.roll(values, width - HD // 2, 1)
    behind = pltpu.roll(values, HD // 2, 1)
    return jnp.where(lane % HD < HD // 2, ahead, behind)


def stack_heads(rows):
    lane = lax.broadcasted_iota(jnp.int32, rows.shape, 1)
    zero = jnp.zeros_like(rows)
    count = rows.shape[1] // HD
    return jnp.concatenate([jnp.where(lane // HD == h, rows, zero) for h in range(count)], axis=0)


def allowed_block(key_segs, query_segs, key_begin, query_begin, count):
    rows, cols = key_segs.shape[0], query_segs.shape[1]
    key_index = key_begin + lax.broadcasted_iota(jnp.int32, (rows, cols), 0)
    query_index = query_begin + lax.broadcasted_iota(jnp.int32, (rows, cols), 1)
    keep = (key_segs == query_segs) & (key_index <= query_index)
    bias = jnp.where(keep, 0.0, NEG_FILL)
    return jnp.concatenate([bias] * count, axis=1)


def forward_kernel(
    info_ref, q_ref, k_ref, v_ref, segq_ref, segk_ref, out_ref, lse_ref, score_ref, acc_ref
):
    i = pl.program_id(0)
    member = info_ref[0]
    heads = q_ref.shape[1] // HD
    stacked = stack_heads(q_ref[...] * jnp.asarray(HD ** (-0.5), BF16))
    begin = info_ref[1 + i]
    wide = heads * BLOCK

    def score_step(j, high):
        base = pl.multiple_of(j * BLOCK, BLOCK)
        keys = k_ref[pl.ds(pl.multiple_of((j ^ member) * BLOCK, BLOCK), BLOCK), :]
        scores = dot_nt(keys, stacked)
        scores = scores + allowed_block(
            segk_ref[pl.ds(base, BLOCK), :1], segq_ref[0], base, i * BLOCK, heads
        )
        score_ref[pl.ds(base, BLOCK), :] = scores
        return jnp.maximum(high, jnp.max(scores, axis=0, keepdims=True))

    high = lax.fori_loop(begin, i + 1, score_step, jnp.full((1, wide), NEG_FILL, F32))
    acc_ref[...] = jnp.zeros_like(acc_ref)

    def value_step(j, total):
        base = pl.multiple_of(j * BLOCK, BLOCK)
        expos = jnp.exp(score_ref[pl.ds(base, BLOCK), :] - high)
        values = v_ref[pl.ds(pl.multiple_of((j ^ member) * BLOCK, BLOCK), BLOCK), :]
        acc_ref[...] += dot_tn(values, expos.astype(BF16))
        return total + jnp.sum(expos, axis=0, keepdims=True)

    total = lax.fori_loop(begin, i + 1, value_step, jnp.zeros((1, wide), F32))
    scaled = acc_ref[...] / total
    pieces = [scaled[h * HD : (h + 1) * HD, h * BLOCK : (h + 1) * BLOCK] for h in range(heads)]
    out_ref[...] = jnp.transpose(jnp.concatenate(pieces, axis=0), (1, 0)).astype(BF16)
    lse_ref[0] = high + jnp.log(total)


def attend_forward(q, k, v, seg_row, seg_col, info):
    length, width = q.shape
    heads = width // HD
    blocks = length // BLOCK
    part = pl.BlockSpec((BLOCK, width), lambda i, info: (i ^ info[0], 0))
    whole = pl.BlockSpec((length, width), lambda i, info: (0, 0))
    return pl.pallas_call(
        forward_kernel,
        grid_spec=pltpu.PrefetchScalarGridSpec(
            num_scalar_prefetch=1,
            grid=(blocks,),
            in_specs=[
                part,
                whole,
                whole,
                pl.BlockSpec((1, 1, BLOCK), lambda i, info: (i, 0, 0)),
                pl.BlockSpec((length, 128), lambda i, info: (0, 0)),
            ],
            out_specs=[part, pl.BlockSpec((1, 1, heads * BLOCK), lambda i, info: (i, 0, 0))],
            scratch_shapes=[
                pltpu.VMEM((length, heads * BLOCK), F32),
                pltpu.VMEM((width, heads * BLOCK), F32),
            ],
        ),
        out_shape=[
            jax.ShapeDtypeStruct((length, width), BF16),
            jax.ShapeDtypeStruct((blocks, 1, heads * BLOCK), F32),
        ],
        cost_estimate=SMALL,
        name="attend_forward",
    )(info, q, k, v, seg_row, seg_col)


def backward_kernel(
    info_ref,
    q_ref,
    k_ref,
    v_ref,
    grad_ref,
    out_ref,
    lse_ref,
    cos_ref,
    sin_ref,
    segq_ref,
    segk_ref,
    d_ref,
    dk_acc,
    dv_acc,
    dq_acc,
):
    i = pl.program_id(0)
    member = info_ref[0]
    width = q_ref.shape[1]
    heads = width // HD
    factor = HD ** (-0.5)

    @pl.when(i == 0)
    def _():
        dk_acc[...] = jnp.zeros_like(dk_acc)
        dv_acc[...] = jnp.zeros_like(dv_acc)

    stacked = stack_heads(q_ref[...] * jnp.asarray(factor, BF16))
    grads = grad_ref[...]
    grad_stacked = stack_heads(grads)
    product = jnp.transpose(grads.astype(F32) * out_ref[...].astype(F32), (1, 0))
    inner = jnp.concatenate(
        [
            jnp.sum(product[h * HD : (h + 1) * HD, :], axis=0, keepdims=True)
            for h in range(heads)
        ],
        axis=1,
    )
    log_sum = lse_ref[0]
    dq_acc[...] = jnp.zeros_like(dq_acc)

    def step(j, carry):
        base = pl.multiple_of(j * BLOCK, BLOCK)
        here = pl.multiple_of((j ^ member) * BLOCK, BLOCK)
        keys = k_ref[pl.ds(here, BLOCK), :]
        values = v_ref[pl.ds(here, BLOCK), :]
        scores = dot_nt(keys, stacked)
        scores = scores + allowed_block(
            segk_ref[pl.ds(base, BLOCK), :1], segq_ref[0], base, i * BLOCK, heads
        )
        probs = jnp.exp(scores - log_sum)
        dv_acc[pl.ds(base, BLOCK), :] += dot_nn(probs.astype(BF16), grad_stacked)
        grad_probs = dot_nt(values, grad_stacked)
        grad_scores = (probs * (grad_probs - inner)).astype(BF16)
        dk_acc[pl.ds(base, BLOCK), :] += dot_nn(grad_scores, stacked)
        dq_acc[...] += dot_tn(keys, grad_scores)
        return carry

    lax.fori_loop(info_ref[1 + i], i + 1, step, 0)

    def unrotate(values, base):
        values = values.astype(BF16).astype(F32)
        cosine = jnp.concatenate([cos_ref[pl.ds(base, BLOCK), :]] * (width // 128), axis=1)
        sine = jnp.concatenate([sin_ref[pl.ds(base, BLOCK), :]] * (width // 128), axis=1)
        return (values * cosine - swap_halves(values) * sine).astype(BF16)

    pieces = [dq_acc[h * HD : (h + 1) * HD, h * BLOCK : (h + 1) * BLOCK] for h in range(heads)]
    dq = jnp.transpose(jnp.concatenate(pieces, axis=0), (1, 0)) * factor
    here = pl.multiple_of((i ^ member) * BLOCK, BLOCK)
    d_ref[pl.ds(here, BLOCK), :width] = unrotate(dq, pl.multiple_of(i * BLOCK, BLOCK))

    @pl.when(i == pl.num_programs(0) - 1)
    def _():
        for j in range(k_ref.shape[0] // BLOCK):
            there = pl.multiple_of((j ^ member) * BLOCK, BLOCK)
            rows = slice(j * BLOCK, (j + 1) * BLOCK)
            d_ref[pl.ds(there, BLOCK), width : 2 * width] = unrotate(dk_acc[rows, :], j * BLOCK)
            d_ref[pl.ds(there, BLOCK), 2 * width :] = dv_acc[rows, :].astype(BF16)


def attend_backward(q, k, v, grads, outs, lse, cosine, sine, seg_row, seg_col, info):
    length, width = q.shape
    heads = width // HD
    blocks = length // BLOCK
    part = pl.BlockSpec((BLOCK, width), lambda i, info: (i ^ info[0], 0))
    whole = pl.BlockSpec((length, width), lambda i, info: (0, 0))
    return pl.pallas_call(
        backward_kernel,
        grid_spec=pltpu.PrefetchScalarGridSpec(
            num_scalar_prefetch=1,
            grid=(blocks,),
            in_specs=[
                part,
                whole,
                whole,
                part,
                part,
                pl.BlockSpec((1, 1, heads * BLOCK), lambda i, info: (i, 0, 0)),
                pl.BlockSpec((length, 128), lambda i, info: (0, 0)),
                pl.BlockSpec((length, 128), lambda i, info: (0, 0)),
                pl.BlockSpec((1, 1, BLOCK), lambda i, info: (i, 0, 0)),
                pl.BlockSpec((length, 128), lambda i, info: (0, 0)),
            ],
            out_specs=pl.BlockSpec((length, 3 * width), lambda i, info: (0, 0)),
            scratch_shapes=[
                pltpu.VMEM((length, width), F32),
                pltpu.VMEM((length, width), F32),
                pltpu.VMEM((width, heads * BLOCK), F32),
            ],
        ),
        out_shape=jax.ShapeDtypeStruct((length, 3 * width), BF16),
        cost_estimate=SMALL,
        name="attend_backward",
    )(info, q, k, v, grads, outs, lse, cosine, sine, seg_row, seg_col)


def choose(refs, want, rows=None, cols=None):
    rows = slice(None) if rows is None else rows
    cols = slice(None) if cols is None else cols
    value = refs[0][rows, cols]
    for k in range(1, len(refs)):
        value = jnp.where(want == k, refs[k][rows, cols], value)
    return value


def small_call(kernel, info, arrays, out_shapes, name):
    return pl.pallas_call(
        kernel,
        grid_spec=pltpu.PrefetchScalarGridSpec(
            num_scalar_prefetch=1,
            grid=(1,),
            in_specs=[
                pl.BlockSpec(a.shape, lambda i, info, n=a.ndim: (0,) * n) for a in arrays
            ],
            out_specs=[
                pl.BlockSpec(o.shape, lambda i, info, n=len(o.shape): (0,) * n)
                for o in out_shapes
            ],
        ),
        out_shape=out_shapes,
        cost_estimate=SMALL,
        name=name,
    )(info, *arrays)


def assemble_cols(pieces, info, groups, dtype):
    rows, w = pieces[0].shape[0], pieces[0].shape[1] // groups

    def kernel(info_ref, *refs):
        for g in range(groups):
            for m in range(4):
                value = choose(refs[:4], info_ref[0] ^ m, cols=slice(g * w, (g + 1) * w))
                refs[4 + g][:, m * w : (m + 1) * w] = value.astype(dtype)

    shapes = [jax.ShapeDtypeStruct((rows, 4 * w), dtype) for _ in range(groups)]
    return small_call(kernel, info, pieces, shapes, "assemble_cols")


def assemble_rows(pieces, info, dtype):
    rows, w = pieces[0].shape

    def kernel(info_ref, *refs):
        for m in range(4):
            refs[4][m * rows : (m + 1) * rows, :] = choose(refs[:4], info_ref[0] ^ m).astype(dtype)

    return small_call(
        kernel, info, pieces, [jax.ShapeDtypeStruct((4 * rows, w), dtype)], "assemble_rows"
    )[0]


def split_cols(array, info):
    rows, w = array.shape[0], array.shape[1] // 4

    def kernel(info_ref, ref, *outs):
        for k in range(4):
            value = ref[:, :w]
            for m in range(1, 4):
                value = jnp.where((info_ref[0] ^ k) == m, ref[:, m * w : (m + 1) * w], value)
            outs[k][...] = value

    shapes = [jax.ShapeDtypeStruct((rows, w), array.dtype) for _ in range(4)]
    return small_call(kernel, info, [array], shapes, "split_cols")


def split_rows(array, info, low, high):
    rows = array.shape[0] // 4

    def kernel(info_ref, ref, *outs):
        for k in range(4):
            start = pl.multiple_of((info_ref[0] ^ k) * rows, rows)
            outs[k][...] = ref[pl.ds(start, rows), low:high]

    shapes = [jax.ShapeDtypeStruct((rows, high - low), array.dtype) for _ in range(4)]
    return small_call(kernel, info, [array], shapes, "split_rows")


def collect(pieces, slots, places, cuts):
    cols, count = pieces[0].shape[1], slots.shape[0]

    def kernel(slot_ref, *refs):
        ins, outs = refs[: len(pieces)], refs[len(pieces) :]
        for ref, (p, row, size) in zip(ins, places):
            for out, (low, high) in zip(outs, cuts):
                begin, end = max(low, row), min(high, row + size)
                if begin < end:
                    out[slot_ref[p], begin - low : end - low, :] = ref[begin - row : end - row, :]

    shapes = [jax.ShapeDtypeStruct((count, high - low, cols), pieces[0].dtype) for low, high in cuts]
    return small_call(kernel, slots, pieces, shapes, "collect")


def take_hidden(gate, up, info, count):
    rows, full = gate.shape
    w = full // count // 4

    def kernel(info_ref, gate_ref, up_ref, out_ref):
        for m in range(4):

            @pl.when(info_ref[0] == m)
            def _(m=m):
                for n, ref in enumerate((gate_ref, up_ref)):
                    for f in range(count):
                        at, low = (n * count + f) * w, (4 * f + m) * w
                        out_ref[:, at : at + w] = ref[:, low : low + w]

    shape = jax.ShapeDtypeStruct((rows, full // 2), gate.dtype)
    return small_call(kernel, info, [gate, up], [shape], "take_hidden")[0]


def restore_hidden(pieces, info, count):
    rows, both = pieces[0].shape
    w = both // 2 // count

    def kernel(info_ref, *refs):
        for m in range(4):
            value = choose(refs[:4], info_ref[0] ^ m).astype(F32)
            for n in range(2):
                for f in range(count):
                    at, low = (n * count + f) * w, (4 * f + m) * w
                    refs[4 + n][:, low : low + w] = value[:, at : at + w]

    shapes = [jax.ShapeDtypeStruct((rows, 2 * both), F32) for _ in range(2)]
    return small_call(kernel, info, pieces, shapes, "restore_hidden")


def prepare_kernel(info_ref, adapter_ref, q_ref, k_ref, v_ref, o_ref, *refs):
    gains, first_ref, second_ref = refs[:4], refs[4], refs[5]
    rows, quarter = adapter_ref.shape
    first_ref[:rows, :] = adapter_ref[...]
    first_ref[rows:, :] = jnp.zeros((first_ref.shape[0] - rows, quarter), BF16)
    size = gains[0].shape[1]
    for g in range(4):
        first_ref[rows + g : rows + g + 1, :size] = gains[g][...]
    for n, ref in enumerate((q_ref, k_ref, v_ref, o_ref)):
        second_ref[:, n * quarter : (n + 1) * quarter] = ref[...]


def prepare(info, adapter, weights, gains):
    quarter = adapter.shape[1] // 4
    rows = weights[0].shape[0]
    own = lambda i, info: (0, info[0])
    return pl.pallas_call(
        prepare_kernel,
        grid_spec=pltpu.PrefetchScalarGridSpec(
            num_scalar_prefetch=1,
            grid=(1,),
            in_specs=[pl.BlockSpec((adapter.shape[0], quarter), own)]
            + [pl.BlockSpec((rows, quarter), own) for _ in weights]
            + [pl.BlockSpec((1, rows), lambda i, info: (0, 0)) for _ in gains],
            out_specs=[
                pl.BlockSpec((adapter.shape[0] + 8, quarter), lambda i, info: (0, 0)),
                pl.BlockSpec((rows, 4 * quarter), lambda i, info: (0, 0)),
            ],
        ),
        out_shape=[
            jax.ShapeDtypeStruct((adapter.shape[0] + 8, quarter), BF16),
            jax.ShapeDtypeStruct((rows, 4 * quarter), BF16),
        ],
        cost_estimate=SMALL,
        name="prepare",
    )(info, adapter, *weights, *[g.reshape(1, -1) for g in gains])


def qkv_kernel(
    info_ref,
    p0_ref,
    p1_ref,
    p2_ref,
    p3_ref,
    gain_ref,
    weight_ref,
    cos_ref,
    sin_ref,
    normed_ref,
    q_ref,
    k_ref,
    v_ref,
    stream_ref,
):
    i = pl.program_id(0)
    member = info_ref[0]
    refs = (p0_ref, p1_ref, p2_ref, p3_ref)
    stream = jnp.concatenate([choose(refs, member ^ m).astype(F32) for m in range(4)], axis=1)

    @pl.when(i == 0)
    def _():
        stream_ref[...] = stream

    normed = (stream * inverse_root(stream) * gain_ref[...]).astype(BF16)
    normed_ref[...] = normed
    count, rows, width = weight_ref.shape
    weight = weight_ref[...].reshape(count * rows, width)
    product = dot_nn(normed, weight)
    quarter = width // 3
    cosine = jnp.concatenate([cos_ref[...]] * (quarter // 128), axis=1)
    sine = jnp.concatenate([sin_ref[...]] * (quarter // 128), axis=1)
    for n, ref in enumerate((q_ref, k_ref)):
        values = product[:, n * quarter : (n + 1) * quarter]
        ref[...] = (values * cosine + swap_halves(values) * sine).astype(BF16)
    v_ref[...] = product[:, 2 * quarter :].astype(BF16)


def norm_qkv(pieces, gain, weights, cosine, sine, info):
    length, quarter = pieces[0].shape
    count, rows, _ = weights.shape
    block = pl.BlockSpec((BLOCK, quarter), lambda i, info: (i, 0))
    natural = pl.BlockSpec((BLOCK, 128), lambda i, info: (i ^ info[0], 0))
    small = jax.ShapeDtypeStruct((length, quarter), BF16)
    return pl.pallas_call(
        qkv_kernel,
        grid_spec=pltpu.PrefetchScalarGridSpec(
            num_scalar_prefetch=1,
            grid=(length // BLOCK,),
            in_specs=[
                pl.BlockSpec((BLOCK, quarter), lambda i, info, k=k: (i ^ k, 0)) for k in range(4)
            ]
            + [
                pl.BlockSpec((1, 4 * quarter), lambda i, info: (0, 0)),
                pl.BlockSpec((count, rows, 3 * quarter), lambda i, info: (0, 0, 0)),
                natural,
                natural,
            ],
            out_specs=[
                pl.BlockSpec((BLOCK, 4 * quarter), lambda i, info: (i, 0)),
                block,
                block,
                block,
                pl.BlockSpec((BLOCK, 4 * quarter), lambda i, info: (0, 0)),
            ],
        ),
        out_shape=[
            jax.ShapeDtypeStruct((length, 4 * quarter), BF16),
            small,
            small,
            small,
            jax.ShapeDtypeStruct((BLOCK, 4 * quarter), F32),
        ],
        cost_estimate=SMALL,
        name="norm_qkv",
    )(info, *pieces, gain, weights, cosine, sine)


def assemble_last(pieces, info, cut):
    rows, w = pieces[0].shape

    def kernel(info_ref, *refs):
        for m in range(4):
            value = choose(refs[:4], info_ref[0] ^ m, rows=slice(0, cut))
            refs[4][:, m * w : (m + 1) * w] = value.astype(F32)
        refs[5][...] = sum(ref[cut:, :].astype(F32) for ref in refs[:4])

    shapes = [jax.ShapeDtypeStruct((cut, 4 * w), F32), jax.ShapeDtypeStruct((rows - cut, w), F32)]
    return small_call(kernel, info, pieces, shapes, "assemble_last")


def joined_back(first, others, weights):
    pieces = [first, *others]
    tokens, quarter = first.shape
    blocks = weights[0].shape[0] // 512

    def kernel(*refs):
        total = dot_nt(refs[0][...], refs[4][...])
        for k in range(1, 4):
            total = total + dot_nt(refs[k][...], refs[4 + k][...])
        i = pl.program_id(0)

        @pl.when(i < blocks // 2)
        def _():
            refs[8][...] = total

        @pl.when(i >= blocks // 2)
        def _():
            refs[9][...] = total

    half = blocks // 2
    return pl.pallas_call(
        kernel,
        grid=(blocks,),
        in_specs=[pl.BlockSpec((tokens, quarter), lambda i: (0, 0)) for _ in pieces]
        + [pl.BlockSpec((512, quarter), lambda i: (i, 0)) for _ in weights],
        out_specs=[
            pl.BlockSpec((tokens, 512), lambda i: (0, jnp.minimum(i, half - 1))),
            pl.BlockSpec((tokens, 512), lambda i: (0, jnp.maximum(i - half, 0))),
        ],
        out_shape=[jax.ShapeDtypeStruct((tokens, 512 * half), F32) for _ in range(2)],
        cost_estimate=SMALL,
        name="joined_back",
    )(*pieces, *weights)


class Order:
    def __init__(self):
        self.last = None

    def tie(self, *values):
        if self.last is not None:
            values = lax.optimization_barrier(values + (self.last,))[:-1]
        return values if len(values) > 1 else values[0]

    def land(self, *values):
        values = lax.optimization_barrier(values + (self.last,))[:-1]
        self.last = values[0]
        return values if len(values) > 1 else values[0]

    def mark(self, value):
        self.last = value[0] if isinstance(value, (tuple, list)) else value
        return value

    def flip(self, array, bits):
        return lax.ppermute(self.tie(array), "seq", [(i, i ^ bits) for i in range(4)])

    def swap(self, pieces):
        return [self.flip(pieces[k], k) for k in (1, 2, 3)]


class Ring:
    def __init__(self, count, order):
        places = list(range(count))
        if count == 8:
            places = [0, 2, 4, 6, 7, 5, 3, 1]
        self.count = count
        self.order = order
        table = np.zeros((count, count), np.int32)
        for p, f in enumerate(places):
            table[f] = [places[(p + k) % count] for k in range(count)]
        self.slots = jnp.asarray(table)[lax.axis_index("fsdp")]
        nxt = [(places[i], places[(i + 1) % count]) for i in range(count)]
        self.perm = {1: nxt, -1: [(b, a) for a, b in nxt]}

    def send(self, array, way):
        return lax.ppermute(self.order.tie(array), "fsdp", self.perm[way])


def middle_row(rows):
    return (rows // 2 + 7) // 8 * 8


class Gather:
    def __init__(self, ring, own):
        self.ring, self.own, self.hop = ring, own, 0
        self.last = ring.count // 2
        self.ahead = self.behind = own
        self.pieces, self.places = [own], [(0, 0, own.shape[0])]

    def launch(self):
        self.hop += 1
        rows, half = self.own.shape[0], middle_row(self.own.shape[0])
        ahead, behind, t = self.ahead, self.behind, self.hop
        if t < self.last:
            self.places += [(self.ring.count - t, 0, rows), (t, 0, rows)]
        else:
            ahead, behind = ahead[:half], behind[half:]
            self.places += [(t, 0, half), (t, half, rows - half)]
        self.ahead, self.behind = self.ring.send(ahead, 1), self.ring.send(behind, -1)

    def land(self):
        self.ahead, self.behind = self.ring.order.land(self.ahead, self.behind)
        self.pieces += [self.ahead, self.behind]

    def rest(self):
        while self.hop < self.last - 1:
            self.launch()
            self.land()

    def collect(self, cuts=None):
        cuts = cuts or [(0, self.own.shape[0])]
        return self.ring.order.mark(collect(self.pieces, self.ring.slots, self.places, cuts))


class Scatter:
    def __init__(self, ring, parts):
        self.ring, self.parts, self.hop = ring, parts, 0
        self.last = ring.count // 2
        self.came = None

    def kernel_call(self, offsets, body, came, outs, name):
        ring, parts = self.ring, self.parts
        count = ring.count

        def pick(part, offset):
            return pl.BlockSpec(
                (1,) + part.shape[1:], lambda i, slots: (slots[offset % count], 0, 0)
            )

        arrays, specs = [], []
        for part in parts:
            for offset in offsets:
                arrays.append(part)
                specs.append(pick(part, offset))
        for array in came:
            arrays.append(array)
            specs.append(pl.BlockSpec(array.shape, lambda i, slots: (0, 0)))
        return pl.pallas_call(
            lambda slots_ref, *refs: body(refs),
            grid_spec=pltpu.PrefetchScalarGridSpec(
                num_scalar_prefetch=1,
                grid=(1,),
                in_specs=specs,
                out_specs=[pl.BlockSpec(o, lambda i, slots: (0, 0)) for o in outs],
            ),
            out_shape=[jax.ShapeDtypeStruct(o, BF16) for o in outs],
            cost_estimate=SMALL,
            name=name,
        )(ring.slots, *arrays)

    def launch(self):
        self.hop += 1
        order, parts, n = self.ring.order, self.parts, len(self.parts)
        t = self.last + 1 - self.hop
        tops = [middle_row(p.shape[1]) for p in parts]
        if self.hop == 1:
            parts = order.tie(*parts)
            self.parts = parts = list(parts) if n > 1 else [parts]

            def first(refs):
                for p in range(n):
                    refs[n + 2 * p][...] = refs[p][0, : tops[p]]
                    refs[n + 2 * p + 1][...] = refs[p][0, tops[p] :]

            outs = []
            for p, part in enumerate(parts):
                outs += [(tops[p], part.shape[2]), (part.shape[1] - tops[p], part.shape[2])]
            send = self.kernel_call([t], first, [], outs, "scatter_first")
        else:

            def middle(refs):
                came, outs = refs[2 * n : 4 * n], refs[4 * n :]
                for p in range(n):
                    for way in range(2):
                        local, got = refs[2 * p + way], came[2 * p + way]
                        rows = slice(0, local.shape[1])
                        if self.hop == 2:
                            rows = slice(0, tops[p]) if way == 0 else slice(tops[p], rows.stop)
                            outs[2 * p + way][...] = local[0]
                        outs[2 * p + way][rows, :] = (
                            local[0, rows].astype(F32) + got[...].astype(F32)
                        ).astype(BF16)

            outs = []
            for part in parts:
                outs += [part.shape[1:]] * 2
            send = self.kernel_call([t, -t], middle, self.came, outs, "scatter_add")
        order.mark(send)
        self.came = [self.ring.send(array, 1 - 2 * (i % 2)) for i, array in enumerate(send)]

    def land(self):
        self.came = list(self.ring.order.land(*self.came))

    def total(self):
        n = len(self.parts)

        def body(refs):
            for p in range(n):
                near = refs[n + 2 * p][...].astype(F32) + refs[n + 2 * p + 1][...].astype(F32)
                refs[3 * n + p][...] = (refs[p][0].astype(F32) + near).astype(BF16)

        outs = [part.shape[1:] for part in self.parts]
        return self.ring.order.mark(self.kernel_call([0], body, self.came, outs, "scatter_sum"))


def per_device(
    latent,
    embed,
    seg_ids,
    positions,
    adapter_weight,
    query_weight,
    key_weight,
    value_weight,
    out_weight,
    gate_weight,
    up_weight,
    down_weight,
    gain_one,
    gain_two,
    gain_three,
    gain_four,
    cotangent,
):
    member = lax.axis_index("seq")
    count = lax.axis_size("fsdp")
    order = Order()
    ring = Ring(count, order)
    tokens, width = latent.shape[1], latent.shape[2]
    length = tokens * 4
    quarter = width // 4
    rows = query_weight.shape[0]
    adapter_rows = adapter_weight.shape[0]
    hidden_rows = down_weight.shape[0] // 4
    hidden_width = hidden_rows * count
    two = 2 * tokens

    def stack(*pieces):
        return jnp.concatenate(pieces, axis=0)

    def shares(part):
        return part.reshape(count, part.shape[0] // count, part.shape[1])

    def low(array):
        return array.astype(BF16)

    def high(array):
        return array.astype(F32)

    who = jnp.full((1,), member, jnp.int32)

    first_own, second_own = prepare(
        who,
        adapter_weight,
        (query_weight, key_weight, value_weight, out_weight),
        (gain_one, gain_two, gain_three, gain_four),
    )
    order.mark(first_own)
    joined = jnp.concatenate([latent[0], embed[0]], axis=1)
    order.mark(joined)
    adapters = Gather(ring, first_own)
    adapters.launch()
    joined_across, joined_beside = order.flip(joined, 2), order.flip(joined, 1)

    gate_up_own = order.mark(take_hidden(*order.tie(gate_weight, up_weight), who, count))
    adapters.land()
    adapters.launch()
    segments = order.tie(seg_ids)[0]
    starts = jnp.sum((segments[None, :] < segments[:, None]).astype(jnp.int32), axis=1)
    places = (jnp.arange(length, dtype=jnp.int32) - starts).astype(F32)
    info = jnp.concatenate([who, starts[::BLOCK] // BLOCK])
    lane = np.arange(128) % HD
    frequency = ROPE_BASE ** (-2.0 * jnp.asarray(lane % (HD // 2), F32) / HD)
    angles = places[:, None] * frequency[None, :]
    cosine = jnp.cos(angles)
    sine = jnp.sin(angles) * jnp.asarray(np.where(lane < HD // 2, -1.0, 1.0), F32)
    seg_row = segments.reshape(length // BLOCK, 1, BLOCK)
    seg_col = jnp.broadcast_to(segments[:, None], (length, 128))
    cosine, sine, seg_col, seg_row, info = order.land(cosine, sine, seg_col, seg_row, info)
    down_own = lax.dynamic_slice_in_dim(
        order.tie(down_weight), member * hidden_rows, hidden_rows, 0
    )
    order.mark(down_own)
    adapters.land()
    adapters.launch()
    adapters.land()
    adapters.launch()
    qkvo = Gather(ring, second_own)
    qkvo.launch()
    joined_beside = order.land(joined_beside)
    joined_near = order.mark(stack(joined, joined_beside))
    adapters.land()
    adapter_cols, gains = adapters.collect([(0, adapter_rows), (adapter_rows, adapter_rows + 8)])
    adapter_cols = adapter_cols.reshape(2 * width, quarter)
    gain_a, gain_b, gain_c, gain_d = [
        high(gains[:, g, :rows].reshape(1, width)) for g in range(4)
    ]
    qkvo.land()
    qkvo.launch()
    stream_near = order.mark(low(dot_nn(order.tie(joined_near), adapter_cols)))
    joined_across = order.land(joined_across)
    joined_diagonal = order.flip(joined_across, 1)
    joined_diagonal = order.land(joined_diagonal)
    joined_far = order.mark(stack(joined_across, joined_diagonal))
    stream_far = order.mark(low(dot_nn(joined_far, adapter_cols)))
    stream_cols = order.mark(stack(stream_near, stream_far))
    stream_across, stream_beside = order.flip(stream_cols, 2), order.flip(stream_cols, 1)
    qkvo.land()
    qkvo.launch()
    qkvo.land()
    qkvo.launch()
    gate_up, down = Gather(ring, gate_up_own), Gather(ring, down_own)
    gate_up.launch()
    down.launch()
    stream_beside, stream_across = order.land(stream_beside, stream_across)
    stream_diagonal = order.flip(stream_across, 1)
    adapter_across, adapter_beside = order.flip(adapter_cols, 2), order.flip(adapter_cols, 1)
    qkvo.land()
    qkvo_full = qkvo.collect()[0]
    stream_diagonal = order.land(stream_diagonal)

    normed_one, q_rows, k_rows, v_rows, stream = norm_qkv(
        [stream_cols, stream_beside, stream_across, stream_diagonal],
        gain_a,
        order.tie(qkvo_full),
        cosine,
        sine,
        who,
    )
    order.mark(q_rows)
    out_sent = split_rows(order.tie(qkvo_full).reshape(width, width), who, 3 * quarter, width)
    order.mark(out_sent)
    out_came = order.swap(out_sent)
    attended, lse = attend_forward(order.tie(q_rows), k_rows, v_rows, seg_row, seg_col, info)
    order.mark(attended)
    out_came = order.land(*out_came)
    out_rows = order.mark(assemble_cols([out_sent[0], *out_came], who, 1, BF16)[0])
    gate_up.land()
    down.land()
    gate_up.launch()
    down.launch()

    def scatter_seq(make, fill=None):
        far = order.mark(make(1))
        diagonal = order.land(order.flip(low(far[tokens:]), 1))
        crossing = order.mark(low(far[:tokens] + high(diagonal)))
        crossing = order.flip(crossing, 2)
        near = order.mark(make(0))
        beside = order.flip(low(near[tokens:]), 1)
        if fill is not None:
            fill()
        beside, crossing = order.land(beside, crossing)
        return near[:tokens] + high(beside) + high(crossing)

    def hop(*rings):
        for r in rings:
            r.land()
        for r in rings:
            r.launch()

    branch = scatter_seq(
        lambda n: dot_nn(order.tie(attended)[n * two : (n + 1) * two], out_rows),
        lambda: hop(gate_up, down),
    )
    resid_one = branch + stream
    root_two = inverse_root(resid_one)
    middle = resid_one * root_two * gain_b
    root_three = inverse_root(middle)
    normed_own = order.mark(low(middle * root_three * gain_c))

    def gather_seq(own, fill=None, near=None):
        across, beside = order.flip(own, 2), order.flip(own, 1)
        beside = order.land(beside)
        close = order.mark(stack(own, beside))
        if fill is not None:
            fill()
        done = near(close) if near is not None else None
        across = order.land(across)
        diagonal = order.land(order.flip(across, 1))
        return close, order.mark(stack(across, diagonal)), done

    normed_near, normed_far, _ = gather_seq(normed_own, lambda: hop(gate_up, down))
    gate_up.land()
    down.land()
    gate_up_full = gate_up.collect()[0].reshape(width, 2 * hidden_width)
    down_full = down.collect()[0].reshape(hidden_width, width)
    adapter_across = order.land(adapter_across)
    adapter_diagonal = order.flip(adapter_across, 1)
    normed_three = [normed_near, normed_far]
    gate_act, up_act, hidden = [], [], []
    for n in range(2):
        act = dot_nn(order.tie(normed_three[n]), gate_up_full)
        gate_act.append(act[:, :hidden_width])
        up_act.append(act[:, hidden_width:])
        hidden.append(low(gate_act[n] / (1.0 + jnp.exp(-gate_act[n])) * up_act[n]))
        order.mark(hidden[n])
    resid_two = scatter_seq(lambda n: dot_nn(order.tie(hidden[n]), down_full)) + middle
    root_four = inverse_root(resid_two)

    upstream = high(cotangent[0])
    d_resid_two = norm_back(resid_two, root_four, upstream * gain_d)
    d_mlp_own = order.mark(low(d_resid_two))
    kept = {}

    def outputs():
        kept["result"] = low(resid_two * root_four * gain_d)
        kept["gain_four"] = jnp.sum(upstream * resid_two * root_four, axis=0)
        order.last = order.land(kept["result"], kept["gain_four"])[0]

    def through_hidden(n, d_mlp):
        d_hidden = dot_nt(order.tie(d_mlp), down_full)
        gate, sigmoid = gate_act[n], 1.0 / (1.0 + jnp.exp(-gate_act[n]))
        d_gate = low(d_hidden * up_act[n] * sigmoid * (1.0 + gate * (1.0 - sigmoid)))
        d_up = low(d_hidden * (gate * sigmoid))
        return order.mark(jnp.concatenate([d_gate, d_up], axis=1))

    d_near, d_far, d_gate_up_near = gather_seq(
        d_mlp_own, outputs, lambda d_mlp: through_hidden(0, d_mlp)
    )
    d_gate_up = [d_gate_up_near, through_hidden(1, d_far)]
    rings = {}

    def hidden_grads():
        down_part = low(dot_tn(order.tie(hidden[0]), d_near) + dot_tn(hidden[1], d_far))
        order.mark(down_part)
        gate_up_part = low(
            dot_tn(order.tie(normed_near), d_gate_up[0]) + dot_tn(normed_far, d_gate_up[1])
        )
        order.mark(gate_up_part)
        rings["hidden"] = Scatter(ring, [shares(down_part), shares(gate_up_part)])
        rings["hidden"].launch()

    d_normed_three = scatter_seq(
        lambda n: dot_nt(order.tie(d_gate_up[n]), gate_up_full), hidden_grads
    )
    d_middle = d_resid_two + norm_back(middle, root_three, d_normed_three * gain_c)
    d_resid_one = norm_back(resid_one, root_two, d_middle * gain_b)
    d_branch_own = order.mark(low(d_resid_one))

    def gain_sums():
        hop(rings["hidden"])
        kept["gain_three"] = jnp.sum(d_normed_three * middle * root_three, axis=0)
        kept["gain_two"] = jnp.sum(d_middle * resid_one * root_two, axis=0)
        order.land(kept["gain_three"], kept["gain_two"])

    d_branch_near, d_branch_far, _ = gather_seq(d_branch_own, gain_sums)
    d_branch = order.mark(stack(d_branch_near, d_branch_far))
    hop(rings["hidden"])
    d_attended = order.mark(low(dot_nt(order.tie(d_branch), out_rows)))
    out_part = order.mark(low(dot_tn(attended, d_branch)))
    out_split = split_cols(order.tie(out_part), who)
    order.mark(out_split)
    out_sums = order.swap(out_split)
    d_qkv = attend_backward(
        q_rows,
        k_rows,
        v_rows,
        order.tie(d_attended),
        attended,
        lse,
        cosine,
        sine,
        seg_row,
        seg_col,
        info,
    )
    order.mark(d_qkv)
    qkv_cols = qkvo_full.reshape(width, width)[:, : 3 * quarter]

    def qkv_grads():
        sums = order.land(*out_sums)
        out_terms = assemble_rows([out_split[0], *sums], who, BF16)
        order.mark(out_terms)
        qkv_part = order.mark(low(dot_tn(order.tie(normed_one), d_qkv)))
        both = jnp.concatenate([shares(qkv_part), shares(out_terms)], axis=2)
        hop(rings["hidden"])
        rings["qkvo"] = Scatter(ring, [both])
        rings["qkvo"].launch()

    d_normed_one = scatter_seq(
        lambda n: dot_nt(order.tie(d_qkv)[n * two : (n + 1) * two], qkv_cols), qkv_grads
    )
    root_one = inverse_root(stream)
    d_stream = low(d_resid_one + norm_back(stream, root_one, d_normed_one * gain_a))
    gain_one_part = jnp.sum(d_normed_one * stream * root_one, axis=0)
    d_split = split_cols(d_stream, who)
    order.mark(d_split)
    d_cols = order.swap(d_split)
    hop(rings["qkvo"])
    d_cols = [d_split[0], *order.land(*d_cols)]
    adapter_part = low(
        dot_tn(joined_near, stack(*d_cols[:2])) + dot_tn(joined_far, stack(*d_cols[2:]))
    )
    gain_parts = jnp.stack([gain_one_part, kept["gain_two"], kept["gain_three"], kept["gain_four"]])
    gain_parts = jnp.transpose(gain_parts.reshape(4, count, rows), (1, 0, 2))
    gain_parts = low(jnp.pad(gain_parts, ((0, 0), (0, 4), (0, quarter - rows))))
    adapter_part = jnp.concatenate([shares(adapter_part), gain_parts], axis=1)
    order.mark(adapter_part)
    rings["adapter"] = Scatter(ring, [adapter_part])
    rings["adapter"].launch()
    rings["hidden"].land()
    down_total, gate_up_total = rings["hidden"].total()

    def exchange(total):
        return total, order.flip(total, 1), order.flip(total, 2)

    def settle(pieces):
        beside, across = order.land(*pieces[1:])
        return [pieces[0], beside, across, order.flip(across, 1)]

    down_done, gate_up_done = exchange(down_total), exchange(gate_up_total)
    hop(rings["adapter"], rings["qkvo"])
    adapter_beside, adapter_diagonal = order.land(adapter_beside, adapter_diagonal)
    latent_grad, embed_grad = joined_back(
        order.tie(d_split[0]),
        d_split[1:],
        [adapter_cols, adapter_beside, adapter_across, adapter_diagonal],
    )
    order.mark(latent_grad)
    hop(rings["adapter"], rings["qkvo"])
    down_done, gate_up_done = settle(down_done), settle(gate_up_done)
    rings["qkvo"].land()
    qkvo_total = rings["qkvo"].total()[0]
    qkvo_done = exchange(qkvo_total)
    hop(rings["adapter"])
    order.land(down_done[3], gate_up_done[3])
    down_grad = assemble_rows([order.tie(down_done[0]), *down_done[1:]], who, F32)
    order.mark(down_grad)
    gate_grad, up_grad = restore_hidden(
        [order.tie(gate_up_done[0]), *gate_up_done[1:]], who, count
    )
    order.mark(gate_grad)
    rings["adapter"].land()
    last_done = exchange(rings["adapter"].total()[0])
    qkvo_done = settle(qkvo_done)
    last_done = settle(last_done)
    query_grad, key_grad, value_grad, out_grad = assemble_cols(
        [order.tie(qkvo_done[0]), *qkvo_done[1:]], who, 4, F32
    )
    order.mark(query_grad)
    last_done[3] = order.land(last_done[3])
    adapter_grad, gain_grads = assemble_last(last_done, who, adapter_rows)
    gain_grads = gain_grads[:, :rows]
    return (
        kept["result"][None],
        latent_grad[None],
        embed_grad[None],
        adapter_grad,
        query_grad,
        key_grad,
        value_grad,
        out_grad,
        gate_grad,
        up_grad,
        down_grad,
        gain_grads[0],
        gain_grads[1],
        gain_grads[2],
        gain_grads[3],
    )


def solution(mesh):
    rows, vector = P("fsdp", None), P("fsdp")
    tokens = P("fsdp", "seq", None)
    placed = (tokens, tokens, rows, P("fsdp", "seq")) + (rows,) * 8 + (vector,) * 4 + (tokens,)
    return jax.shard_map(
        per_device,
        mesh=mesh,
        in_specs=placed,
        out_specs=(tokens,) * 3 + (rows,) * 8 + (vector,) * 4,
        check_vma=False,
    )
```

```python
import jax
import jax.numpy as jnp
import numpy as np
from jax import lax
from jax.experimental import pallas as pl
from jax.experimental.pallas import tpu as pltpu
from jax.sharding import PartitionSpec as P

H = 16
HD = 64
EPSILON = 1e-06
ROPE_BASE = 50000.0
NEG_FILL = -1e30
BLOCK = 256
F32 = jnp.float32
SMALL = pl.CostEstimate(flops=1, bytes_accessed=1, transcendentals=0)
LONG = pl.CostEstimate(flops=10**11, bytes_accessed=1, transcendentals=0)
BF16 = jnp.bfloat16


def dot_nn(left, right):
    return lax.dot_general(left, right, (((1,), (0,)), ((), ())), preferred_element_type=F32)


def dot_tn(left, right):
    return lax.dot_general(left, right, (((0,), (0,)), ((), ())), preferred_element_type=F32)


def dot_nt(left, right):
    return lax.dot_general(left, right, (((1,), (1,)), ((), ())), preferred_element_type=F32)


def inverse_root(values):
    return lax.rsqrt(jnp.mean(values * values, axis=-1, keepdims=True) + EPSILON)


def norm_back(values, root, upstream):
    inner_mean = jnp.mean(upstream * values, axis=-1, keepdims=True)
    return root * upstream - values * root * root * root * inner_mean


def swap_halves(values):
    lane = lax.broadcasted_iota(jnp.int32, values.shape, 1)
    width = values.shape[1]
    ahead = pltpu.roll(values, width - HD // 2, 1)
    behind = pltpu.roll(values, HD // 2, 1)
    return jnp.where(lane % HD < HD // 2, ahead, behind)


def stack_heads(rows):
    lane = lax.broadcasted_iota(jnp.int32, rows.shape, 1)
    zero = jnp.zeros_like(rows)
    count = rows.shape[1] // HD
    return jnp.concatenate([jnp.where(lane // HD == h, rows, zero) for h in range(count)], axis=0)


def allowed_block(key_segs, query_segs, key_begin, query_begin, count):
    rows, cols = key_segs.shape[0], query_segs.shape[1]
    key_index = key_begin + lax.broadcasted_iota(jnp.int32, (rows, cols), 0)
    query_index = query_begin + lax.broadcasted_iota(jnp.int32, (rows, cols), 1)
    keep = (key_segs == query_segs) & (key_index <= query_index)
    bias = jnp.where(keep, 0.0, NEG_FILL)
    return jnp.concatenate([bias] * count, axis=1)


def forward_kernel(
    info_ref, q_ref, k_ref, v_ref, segq_ref, segk_ref, out_ref, lse_ref, score_ref, acc_ref
):
    i = pl.program_id(0)
    member = info_ref[0]
    heads = q_ref.shape[1] // HD
    stacked = stack_heads(q_ref[...] * jnp.asarray(HD ** (-0.5), BF16))
    begin = info_ref[1 + i]
    wide = heads * BLOCK

    def score_step(j, high):
        base = pl.multiple_of(j * BLOCK, BLOCK)
        keys = k_ref[pl.ds(pl.multiple_of((j ^ member) * BLOCK, BLOCK), BLOCK), :]
        scores = dot_nt(keys, stacked)
        scores = scores + allowed_block(
            segk_ref[pl.ds(base, BLOCK), :1], segq_ref[0], base, i * BLOCK, heads
        )
        score_ref[pl.ds(base, BLOCK), :] = scores
        return jnp.maximum(high, jnp.max(scores, axis=0, keepdims=True))

    high = lax.fori_loop(begin, i + 1, score_step, jnp.full((1, wide), NEG_FILL, F32))
    acc_ref[...] = jnp.zeros_like(acc_ref)

    def value_step(j, total):
        base = pl.multiple_of(j * BLOCK, BLOCK)
        expos = jnp.exp(score_ref[pl.ds(base, BLOCK), :] - high)
        values = v_ref[pl.ds(pl.multiple_of((j ^ member) * BLOCK, BLOCK), BLOCK), :]
        acc_ref[...] += dot_tn(values, expos.astype(BF16))
        return total + jnp.sum(expos, axis=0, keepdims=True)

    total = lax.fori_loop(begin, i + 1, value_step, jnp.zeros((1, wide), F32))
    scaled = acc_ref[...] / total
    pieces = [scaled[h * HD : (h + 1) * HD, h * BLOCK : (h + 1) * BLOCK] for h in range(heads)]
    out_ref[...] = jnp.transpose(jnp.concatenate(pieces, axis=0), (1, 0)).astype(BF16)
    lse_ref[0] = high + jnp.log(total)


def attend_forward(q, k, v, seg_row, seg_col, info):
    length, width = q.shape
    heads = width // HD
    blocks = length // BLOCK
    part = pl.BlockSpec((BLOCK, width), lambda i, info: (i ^ info[0], 0))
    whole = pl.BlockSpec((length, width), lambda i, info: (0, 0))
    return pl.pallas_call(
        forward_kernel,
        grid_spec=pltpu.PrefetchScalarGridSpec(
            num_scalar_prefetch=1,
            grid=(blocks,),
            in_specs=[
                part,
                whole,
                whole,
                pl.BlockSpec((1, 1, BLOCK), lambda i, info: (i, 0, 0)),
                pl.BlockSpec((length, 128), lambda i, info: (0, 0)),
            ],
            out_specs=[part, pl.BlockSpec((1, 1, heads * BLOCK), lambda i, info: (i, 0, 0))],
            scratch_shapes=[
                pltpu.VMEM((length, heads * BLOCK), F32),
                pltpu.VMEM((width, heads * BLOCK), F32),
            ],
        ),
        out_shape=[
            jax.ShapeDtypeStruct((length, width), BF16),
            jax.ShapeDtypeStruct((blocks, 1, heads * BLOCK), F32),
        ],
        cost_estimate=SMALL,
        name="attend_forward",
    )(info, q, k, v, seg_row, seg_col)


def backward_kernel(
    info_ref,
    q_ref,
    k_ref,
    v_ref,
    grad_ref,
    out_ref,
    lse_ref,
    cos_ref,
    sin_ref,
    segq_ref,
    segk_ref,
    d_ref,
    dk_acc,
    dv_acc,
    dq_acc,
):
    i = pl.program_id(0)
    member = info_ref[0]
    width = q_ref.shape[1]
    heads = width // HD
    factor = HD ** (-0.5)

    @pl.when(i == 0)
    def _():
        dk_acc[...] = jnp.zeros_like(dk_acc)
        dv_acc[...] = jnp.zeros_like(dv_acc)

    stacked = stack_heads(q_ref[...] * jnp.asarray(factor, BF16))
    grads = grad_ref[...]
    grad_stacked = stack_heads(grads)
    product = jnp.transpose(grads.astype(F32) * out_ref[...].astype(F32), (1, 0))
    inner = jnp.concatenate(
        [
            jnp.sum(product[h * HD : (h + 1) * HD, :], axis=0, keepdims=True)
            for h in range(heads)
        ],
        axis=1,
    )
    log_sum = lse_ref[0]
    dq_acc[...] = jnp.zeros_like(dq_acc)

    def step(j, carry):
        base = pl.multiple_of(j * BLOCK, BLOCK)
        here = pl.multiple_of((j ^ member) * BLOCK, BLOCK)
        keys = k_ref[pl.ds(here, BLOCK), :]
        values = v_ref[pl.ds(here, BLOCK), :]
        scores = dot_nt(keys, stacked)
        scores = scores + allowed_block(
            segk_ref[pl.ds(base, BLOCK), :1], segq_ref[0], base, i * BLOCK, heads
        )
        probs = jnp.exp(scores - log_sum)
        dv_acc[pl.ds(base, BLOCK), :] += dot_nn(probs.astype(BF16), grad_stacked)
        grad_probs = dot_nt(values, grad_stacked)
        grad_scores = (probs * (grad_probs - inner)).astype(BF16)
        dk_acc[pl.ds(base, BLOCK), :] += dot_nn(grad_scores, stacked)
        dq_acc[...] += dot_tn(keys, grad_scores)
        return carry

    lax.fori_loop(info_ref[1 + i], i + 1, step, 0)

    def unrotate(values, base):
        values = values.astype(BF16).astype(F32)
        cosine = jnp.concatenate([cos_ref[pl.ds(base, BLOCK), :]] * (width // 128), axis=1)
        sine = jnp.concatenate([sin_ref[pl.ds(base, BLOCK), :]] * (width // 128), axis=1)
        return (values * cosine - swap_halves(values) * sine).astype(BF16)

    pieces = [dq_acc[h * HD : (h + 1) * HD, h * BLOCK : (h + 1) * BLOCK] for h in range(heads)]
    dq = jnp.transpose(jnp.concatenate(pieces, axis=0), (1, 0)) * factor
    here = pl.multiple_of((i ^ member) * BLOCK, BLOCK)
    d_ref[pl.ds(here, BLOCK), :width] = unrotate(dq, pl.multiple_of(i * BLOCK, BLOCK))

    @pl.when(i == pl.num_programs(0) - 1)
    def _():
        for j in range(k_ref.shape[0] // BLOCK):
            there = pl.multiple_of((j ^ member) * BLOCK, BLOCK)
            rows = slice(j * BLOCK, (j + 1) * BLOCK)
            d_ref[pl.ds(there, BLOCK), width : 2 * width] = unrotate(dk_acc[rows, :], j * BLOCK)
            d_ref[pl.ds(there, BLOCK), 2 * width :] = dv_acc[rows, :].astype(BF16)


def attend_backward(q, k, v, grads, outs, lse, cosine, sine, seg_row, seg_col, info):
    length, width = q.shape
    heads = width // HD
    blocks = length // BLOCK
    part = pl.BlockSpec((BLOCK, width), lambda i, info: (i ^ info[0], 0))
    whole = pl.BlockSpec((length, width), lambda i, info: (0, 0))
    return pl.pallas_call(
        backward_kernel,
        grid_spec=pltpu.PrefetchScalarGridSpec(
            num_scalar_prefetch=1,
            grid=(blocks,),
            in_specs=[
                part,
                whole,
                whole,
                part,
                part,
                pl.BlockSpec((1, 1, heads * BLOCK), lambda i, info: (i, 0, 0)),
                pl.BlockSpec((length, 128), lambda i, info: (0, 0)),
                pl.BlockSpec((length, 128), lambda i, info: (0, 0)),
                pl.BlockSpec((1, 1, BLOCK), lambda i, info: (i, 0, 0)),
                pl.BlockSpec((length, 128), lambda i, info: (0, 0)),
            ],
            out_specs=pl.BlockSpec((length, 3 * width), lambda i, info: (0, 0)),
            scratch_shapes=[
                pltpu.VMEM((length, width), F32),
                pltpu.VMEM((length, width), F32),
                pltpu.VMEM((width, heads * BLOCK), F32),
            ],
        ),
        out_shape=jax.ShapeDtypeStruct((length, 3 * width), BF16),
        cost_estimate=SMALL,
        name="attend_backward",
    )(info, q, k, v, grads, outs, lse, cosine, sine, seg_row, seg_col)


def choose(refs, want, rows=None, cols=None):
    rows = slice(None) if rows is None else rows
    cols = slice(None) if cols is None else cols
    value = refs[0][rows, cols]
    for k in range(1, len(refs)):
        value = jnp.where(want == k, refs[k][rows, cols], value)
    return value


def small_call(kernel, info, arrays, out_shapes, name):
    return pl.pallas_call(
        kernel,
        grid_spec=pltpu.PrefetchScalarGridSpec(
            num_scalar_prefetch=1,
            grid=(1,),
            in_specs=[
                pl.BlockSpec(a.shape, lambda i, info, n=a.ndim: (0,) * n) for a in arrays
            ],
            out_specs=[
                pl.BlockSpec(o.shape, lambda i, info, n=len(o.shape): (0,) * n)
                for o in out_shapes
            ],
        ),
        out_shape=out_shapes,
        cost_estimate=SMALL,
        name=name,
    )(info, *arrays)


def assemble_cols(pieces, info, groups, dtype):
    rows, w = pieces[0].shape[0], pieces[0].shape[1] // groups

    def kernel(info_ref, *refs):
        for g in range(groups):
            for m in range(4):
                value = choose(refs[:4], info_ref[0] ^ m, cols=slice(g * w, (g + 1) * w))
                refs[4 + g][:, m * w : (m + 1) * w] = value.astype(dtype)

    shapes = [jax.ShapeDtypeStruct((rows, 4 * w), dtype) for _ in range(groups)]
    return small_call(kernel, info, pieces, shapes, "assemble_cols")


def assemble_rows(pieces, info, dtype):
    rows, w = pieces[0].shape

    def kernel(info_ref, *refs):
        for m in range(4):
            refs[4][m * rows : (m + 1) * rows, :] = choose(refs[:4], info_ref[0] ^ m).astype(dtype)

    return small_call(
        kernel, info, pieces, [jax.ShapeDtypeStruct((4 * rows, w), dtype)], "assemble_rows"
    )[0]


def split_cols(array, info):
    rows, w = array.shape[0], array.shape[1] // 4

    def kernel(info_ref, ref, *outs):
        for k in range(4):
            value = ref[:, :w]
            for m in range(1, 4):
                value = jnp.where((info_ref[0] ^ k) == m, ref[:, m * w : (m + 1) * w], value)
            outs[k][...] = value

    shapes = [jax.ShapeDtypeStruct((rows, w), array.dtype) for _ in range(4)]
    return small_call(kernel, info, [array], shapes, "split_cols")


def split_rows(array, info, low, high):
    rows = array.shape[0] // 4

    def kernel(info_ref, ref, *outs):
        for k in range(4):
            start = pl.multiple_of((info_ref[0] ^ k) * rows, rows)
            outs[k][...] = ref[pl.ds(start, rows), low:high]

    shapes = [jax.ShapeDtypeStruct((rows, high - low), array.dtype) for _ in range(4)]
    return small_call(kernel, info, [array], shapes, "split_rows")


def collect(pieces, slots, places, cuts):
    cols, count = pieces[0].shape[1], slots.shape[0]

    def kernel(slot_ref, *refs):
        ins, outs = refs[: len(pieces)], refs[len(pieces) :]
        for ref, (p, row, size) in zip(ins, places):
            for out, (low, high) in zip(outs, cuts):
                begin, end = max(low, row), min(high, row + size)
                if begin < end:
                    out[slot_ref[p], begin - low : end - low, :] = ref[begin - row : end - row, :]

    shapes = [jax.ShapeDtypeStruct((count, high - low, cols), pieces[0].dtype) for low, high in cuts]
    return small_call(kernel, slots, pieces, shapes, "collect")


def hidden_plan(rows, both, hidden_rows, width):
    step = -(-hidden_rows // 16) * 16
    base = both // 128 * rows
    return base, step, base + width // 128 * step


def take_hidden(gate, up, info, count):
    rows, full = gate.shape
    w = full // count // 4

    def kernel(info_ref, gate_ref, up_ref, out_ref):
        for m in range(4):

            @pl.when(info_ref[0] == m)
            def _(m=m):
                for n, ref in enumerate((gate_ref, up_ref)):
                    for f in range(count):
                        at, low = (n * count + f) * w, (4 * f + m) * w
                        out_ref[:, at : at + w] = ref[:, low : low + w]

    shape = jax.ShapeDtypeStruct((rows, full // 2), gate.dtype)
    return small_call(kernel, info, [gate, up], [shape], "take_hidden")[0]


def restore_hidden(packed, rows, both, hidden_rows, width, count):
    total = packed.shape[1]
    base, step, _ = hidden_plan(rows, both, hidden_rows, width)
    w = both // 2 // count

    def kernel(ref, gate_ref, up_ref, down_ref):
        for m in range(4):
            tiles = [ref[m, c * rows : (c + 1) * rows, :] for c in range(both // 128)]
            value = jnp.concatenate(tiles, axis=1).astype(F32)
            for n, out in enumerate((gate_ref, up_ref)):
                for f in range(count):
                    at, low = (n * count + f) * w, (4 * f + m) * w
                    out[:, low : low + w] = value[:, at : at + w]
            for c in range(width // 128):
                at = base + c * step
                part = ref[m, at : at + hidden_rows, :].astype(F32)
                down_ref[m * hidden_rows : (m + 1) * hidden_rows, c * 128 : (c + 1) * 128] = part

    outs = [(rows, 2 * both), (rows, 2 * both), (4 * hidden_rows, width)]
    return pl.pallas_call(
        kernel,
        grid=(1,),
        in_specs=[pl.BlockSpec((4, total, 128), lambda i: (0, 0, 0))],
        out_specs=[pl.BlockSpec(o, lambda i: (0, 0)) for o in outs],
        out_shape=[jax.ShapeDtypeStruct(o, F32) for o in outs],
        cost_estimate=SMALL,
        name="restore_hidden",
    )(packed)


def prepare_kernel(info_ref, adapter_ref, q_ref, k_ref, v_ref, o_ref, *refs):
    gains, first_ref, second_ref = refs[:4], refs[4], refs[5]
    rows, quarter = adapter_ref.shape
    first_ref[:rows, :] = adapter_ref[...]
    first_ref[rows:, :] = jnp.zeros((first_ref.shape[0] - rows, quarter), BF16)
    size = gains[0].shape[1]
    for g in range(4):
        first_ref[rows + g : rows + g + 1, :size] = gains[g][...]
    for n, ref in enumerate((q_ref, k_ref, v_ref, o_ref)):
        second_ref[:, n * quarter : (n + 1) * quarter] = ref[...]


def prepare(info, adapter, weights, gains):
    quarter = adapter.shape[1] // 4
    rows = weights[0].shape[0]
    own = lambda i, info: (0, info[0])
    return pl.pallas_call(
        prepare_kernel,
        grid_spec=pltpu.PrefetchScalarGridSpec(
            num_scalar_prefetch=1,
            grid=(1,),
            in_specs=[pl.BlockSpec((adapter.shape[0], quarter), own)]
            + [pl.BlockSpec((rows, quarter), own) for _ in weights]
            + [pl.BlockSpec((1, rows), lambda i, info: (0, 0)) for _ in gains],
            out_specs=[
                pl.BlockSpec((adapter.shape[0] + 8, quarter), lambda i, info: (0, 0)),
                pl.BlockSpec((rows, 4 * quarter), lambda i, info: (0, 0)),
            ],
        ),
        out_shape=[
            jax.ShapeDtypeStruct((adapter.shape[0] + 8, quarter), BF16),
            jax.ShapeDtypeStruct((rows, 4 * quarter), BF16),
        ],
        cost_estimate=SMALL,
        name="prepare",
    )(info, adapter, *weights, *[g.reshape(1, -1) for g in gains])


def qkv_kernel(
    info_ref,
    p0_ref,
    p1_ref,
    p2_ref,
    p3_ref,
    gain_ref,
    weight_ref,
    cos_ref,
    sin_ref,
    normed_ref,
    q_ref,
    k_ref,
    v_ref,
    stream_ref,
):
    i = pl.program_id(0)
    member = info_ref[0]
    refs = (p0_ref, p1_ref, p2_ref, p3_ref)
    stream = jnp.concatenate([choose(refs, member ^ m).astype(F32) for m in range(4)], axis=1)

    @pl.when(i == 0)
    def _():
        stream_ref[...] = stream

    normed = (stream * inverse_root(stream) * gain_ref[...]).astype(BF16)
    normed_ref[...] = normed
    count, rows, width = weight_ref.shape
    weight = weight_ref[...].reshape(count * rows, width)
    product = dot_nn(normed, weight)
    quarter = width // 3
    cosine = jnp.concatenate([cos_ref[...]] * (quarter // 128), axis=1)
    sine = jnp.concatenate([sin_ref[...]] * (quarter // 128), axis=1)
    for n, ref in enumerate((q_ref, k_ref)):
        values = product[:, n * quarter : (n + 1) * quarter]
        ref[...] = (values * cosine + swap_halves(values) * sine).astype(BF16)
    v_ref[...] = product[:, 2 * quarter :].astype(BF16)


def norm_qkv(pieces, gain, weights, cosine, sine, info):
    length, quarter = pieces[0].shape
    count, rows, _ = weights.shape
    block = pl.BlockSpec((BLOCK, quarter), lambda i, info: (i, 0))
    natural = pl.BlockSpec((BLOCK, 128), lambda i, info: (i ^ info[0], 0))
    small = jax.ShapeDtypeStruct((length, quarter), BF16)
    return pl.pallas_call(
        qkv_kernel,
        grid_spec=pltpu.PrefetchScalarGridSpec(
            num_scalar_prefetch=1,
            grid=(length // BLOCK,),
            in_specs=[
                pl.BlockSpec((BLOCK, quarter), lambda i, info, k=k: (i ^ k, 0)) for k in range(4)
            ]
            + [
                pl.BlockSpec((1, 4 * quarter), lambda i, info: (0, 0)),
                pl.BlockSpec((count, rows, 3 * quarter), lambda i, info: (0, 0, 0)),
                natural,
                natural,
            ],
            out_specs=[
                pl.BlockSpec((BLOCK, 4 * quarter), lambda i, info: (i, 0)),
                block,
                block,
                block,
                pl.BlockSpec((BLOCK, 4 * quarter), lambda i, info: (0, 0)),
            ],
        ),
        out_shape=[
            jax.ShapeDtypeStruct((length, 4 * quarter), BF16),
            small,
            small,
            small,
            jax.ShapeDtypeStruct((BLOCK, 4 * quarter), F32),
        ],
        cost_estimate=SMALL,
        name="norm_qkv",
    )(info, *pieces, gain, weights, cosine, sine)


def assemble_last(pieces, info, cut, size):
    rows, w = pieces[0].shape

    def kernel(info_ref, *refs):
        for m in range(4):
            value = choose(refs[:4], info_ref[0] ^ m, rows=slice(0, cut))
            refs[4][:, m * w : (m + 1) * w] = value.astype(F32)
        total = sum(ref[cut:, :].astype(F32) for ref in refs[:4])
        for g in range(4):
            refs[5 + g][...] = total[g : g + 1, :size]

    shapes = [jax.ShapeDtypeStruct((cut, 4 * w), F32)]
    shapes += [jax.ShapeDtypeStruct((1, size), F32) for _ in range(4)]
    return small_call(kernel, info, pieces, shapes, "assemble_last")


def stream_rows(blocks, weight):
    tokens, quarter, n = blocks[0].shape[0], weight.shape[1], len(blocks)

    def kernel(*refs):
        for k in range(n):
            value = dot_nn(refs[k][...], refs[n][...])
            refs[n + 1][k * tokens : (k + 1) * tokens, :] = value.astype(BF16)

    return pl.pallas_call(
        kernel,
        out_shape=jax.ShapeDtypeStruct((n * tokens, quarter), BF16),
        cost_estimate=SMALL,
        name="stream_rows",
    )(*blocks, weight)


def adapter_terms(blocks, d_cols, gains, count):
    width, quarter, n = blocks[0].shape[1] // 2, d_cols[0].shape[1], len(blocks)
    rows, size = 2 * width // count, width // count

    def kernel(*refs):
        gain_refs, out_ref = refs[2 * n : 2 * n + 4], refs[2 * n + 4]
        out_ref[:, rows:, :] = jnp.zeros((count, 8, quarter), BF16)
        for half in range(2):
            cols = slice(half * width, (half + 1) * width)
            total = dot_tn(refs[0][:, cols], refs[n][...])
            for k in range(1, n):
                total = total + dot_tn(refs[k][:, cols], refs[n + k][...])
            total = total.astype(BF16)
            for f in range(count // 2):
                out_ref[half * count // 2 + f, :rows, :] = total[f * rows : (f + 1) * rows, :]
        for g, ref in enumerate(gain_refs):
            for f in range(count):
                value = ref[:, f * size : (f + 1) * size].astype(BF16)
                out_ref[f, rows + g : rows + g + 1, :size] = value

    return pl.pallas_call(
        kernel,
        out_shape=jax.ShapeDtypeStruct((count, rows + 8, quarter), BF16),
        cost_estimate=SMALL,
        name="adapter_terms",
    )(*blocks, *d_cols, *gains)


def joined_back(first, others, weights):
    pieces = [first, *others]
    tokens, quarter = first.shape
    blocks = weights[0].shape[0] // 512

    def kernel(*refs):
        total = dot_nt(refs[0][...], refs[4][...])
        for k in range(1, 4):
            total = total + dot_nt(refs[k][...], refs[4 + k][...])
        i = pl.program_id(0)

        @pl.when(i < blocks // 2)
        def _():
            refs[8][...] = total

        @pl.when(i >= blocks // 2)
        def _():
            refs[9][...] = total

    half = blocks // 2
    return pl.pallas_call(
        kernel,
        grid=(blocks,),
        in_specs=[pl.BlockSpec((tokens, quarter), lambda i: (0, 0)) for _ in pieces]
        + [pl.BlockSpec((512, quarter), lambda i: (i, 0)) for _ in weights],
        out_specs=[
            pl.BlockSpec((tokens, 512), lambda i: (0, jnp.minimum(i, half - 1))),
            pl.BlockSpec((tokens, 512), lambda i: (0, jnp.maximum(i - half, 0))),
        ],
        out_shape=[jax.ShapeDtypeStruct((tokens, 512 * half), F32) for _ in range(2)],
        cost_estimate=SMALL,
        name="joined_back",
    )(*pieces, *weights)


def rows_call(body, sums, cols, gains, outs, name):
    near, beside, crossing = sums
    tokens, width = beside.shape
    step = tokens // 2
    n = 3 + len(cols) + len(gains)

    def kernel(info_ref, *refs):
        total = refs[0][...] + refs[1][...].astype(F32) + refs[2][...].astype(F32)
        values = [ref[...].astype(F32) for ref in refs[3 : 3 + len(cols)]]
        results = body(info_ref, total, *values, *[ref[...] for ref in refs[3 + len(cols) : n]])
        for ref, value in zip(refs[n:], results):
            if ref.shape[0] == 1:

                @pl.when(pl.program_id(0) == 0)
                def _(ref=ref):
                    ref[...] = jnp.zeros_like(ref)

                ref[...] += jnp.sum(value, axis=0, keepdims=True)
            else:
                ref[...] = value.astype(ref.dtype)

    def spec(cols):
        return pl.BlockSpec((step, cols), lambda i, info: (i, 0))

    fixed = pl.BlockSpec((1, width), lambda i, info: (0, 0))
    shapes, specs = [], []
    for kind in outs:
        wide = width if kind != "split" else width // 4
        if kind == "sum":
            shapes.append(jax.ShapeDtypeStruct((1, width), F32))
            specs.append(fixed)
        else:
            shapes.append(jax.ShapeDtypeStruct((tokens, wide), F32 if kind == "wide" else BF16))
            specs.append(spec(wide))

    def run(info):
        return pl.pallas_call(
            kernel,
            grid_spec=pltpu.PrefetchScalarGridSpec(
                num_scalar_prefetch=1,
                grid=(2,),
                in_specs=[spec(width)] * (3 + len(cols)) + [fixed] * len(gains),
                out_specs=specs,
            ),
            out_shape=shapes,
            cost_estimate=LONG if name == "after_hidden" else SMALL,
            name=name,
        )(info, near, beside, crossing, *cols, *gains)

    return run


def after_branch(info, total, stream, gain_b, gain_c):
    resid = total + stream
    middle = resid * inverse_root(resid) * gain_b
    return resid, middle, middle * inverse_root(middle) * gain_c


def after_mlp(info, total, middle, upstream, gain_d):
    resid = total + middle
    root = inverse_root(resid)
    d_resid = norm_back(resid, root, upstream * gain_d)
    scaled = resid * root
    return d_resid, d_resid, scaled * gain_d, upstream * scaled


def after_hidden(info, d_normed, middle, resid, d_resid_two, gain_b, gain_c):
    root_three, root_two = inverse_root(middle), inverse_root(resid)
    d_middle = d_resid_two + norm_back(middle, root_three, d_normed * gain_c)
    d_resid = norm_back(resid, root_two, d_middle * gain_b)
    return d_resid, d_resid, d_normed * middle * root_three, d_middle * resid * root_two


def after_attention(info, d_normed, stream, d_resid, gain_a):
    root = inverse_root(stream)
    d_stream = d_resid + norm_back(stream, root, d_normed * gain_a)
    w = d_stream.shape[1] // 4
    pieces = []
    for k in range(4):
        value = d_stream[:, :w]
        for m in range(1, 4):
            value = jnp.where((info[0] ^ k) == m, d_stream[:, m * w : (m + 1) * w], value)
        pieces.append(value)
    return (*pieces, d_normed * stream * root)


def hidden_terms(normed, d_acts, hidden, d_mlp, count):
    tokens, width = normed[0].shape
    rows, both, hidden_width = width // count, d_acts[0].shape[1], hidden[0].shape[1]
    hidden_rows = hidden_width // count
    base, step, total = hidden_plan(rows, both, hidden_rows, width)

    def kernel(n0, n1, d0, d1, h0, h1, m0, m1, out_ref):
        def wide(begin, size):
            cols = pl.ds(begin, size)
            part = (dot_tn(n0[...], d0[:, cols]) + dot_tn(n1[...], d1[:, cols])).astype(BF16)
            for h in range(size // 128):
                at = begin // 128 * rows + h * rows
                at = at if isinstance(at, int) else pl.multiple_of(at, rows)
                for f in range(count):
                    out_ref[f, pl.ds(at, rows), :] = part[
                        f * rows : (f + 1) * rows, h * 128 : (h + 1) * 128
                    ]

        def tall(c, carry):
            cols = pl.ds(pl.multiple_of(c * 256, 256), 256)
            part = dot_tn(h0[...], m0[:, cols]) + dot_tn(h1[...], m1[:, cols])
            for h in range(2):
                at = pl.multiple_of(base + (2 * c + h) * step, 16)
                for f in range(count):
                    value = part[f * hidden_rows : (f + 1) * hidden_rows, h * 128 : (h + 1) * 128]
                    if step > hidden_rows:
                        rest = jnp.zeros((step - hidden_rows, 128), F32)
                        value = jnp.concatenate([value, rest], axis=0)
                    out_ref[f, pl.ds(at, step), :] = value.astype(BF16)
            return carry

        def pair(c, carry):
            wide(pl.multiple_of(c * 256, 256), 256)
            return carry

        lax.fori_loop(0, both // 256, pair, 0)
        if both % 256:
            wide(both // 256 * 256, 128)
        lax.fori_loop(0, width // 256, tall, 0)

    arrays = [*normed, *d_acts, *hidden, *d_mlp]
    return pl.pallas_call(
        kernel,
        grid=(1,),
        in_specs=[pl.BlockSpec(a.shape, lambda i: (0, 0)) for a in arrays],
        out_specs=pl.BlockSpec((count, total, 128), lambda i: (0, 0, 0)),
        out_shape=jax.ShapeDtypeStruct((count, total, 128), BF16),
        cost_estimate=SMALL,
        name="hidden_terms",
    )(*arrays)


class Order:
    def __init__(self):
        self.last = None

    def tie(self, *values):
        if self.last is not None:
            values = lax.optimization_barrier(values + (self.last,))[:-1]
        return values if len(values) > 1 else values[0]

    def land(self, *values):
        values = lax.optimization_barrier(values + (self.last,))[:-1]
        self.last = values[0]
        return values if len(values) > 1 else values[0]

    def mark(self, value):
        self.last = value[0] if isinstance(value, (tuple, list)) else value
        return value

    def flip(self, array, bits):
        return lax.ppermute(self.tie(array), "seq", [(i, i ^ bits) for i in range(4)])

    def swap(self, pieces):
        return [self.flip(pieces[k], k) for k in (1, 2, 3)]


class Ring:
    def __init__(self, count, order):
        places = list(range(count))
        if count == 8:
            places = [0, 2, 4, 6, 7, 5, 3, 1]
        self.count = count
        self.order = order
        table = np.zeros((count, count), np.int32)
        for p, f in enumerate(places):
            table[f] = [places[(p + k) % count] for k in range(count)]
        self.slots = jnp.asarray(table)[lax.axis_index("fsdp")]
        nxt = [(places[i], places[(i + 1) % count]) for i in range(count)]
        self.perm = {1: nxt, -1: [(b, a) for a, b in nxt]}

    def send(self, array, way):
        return lax.ppermute(self.order.tie(array), "fsdp", self.perm[way])


def middle_row(rows):
    return (rows // 2 + 7) // 8 * 8


class Gather:
    def __init__(self, ring, own):
        self.ring, self.own, self.hop = ring, own, 0
        self.last = ring.count // 2
        self.ahead = self.behind = own
        self.pieces, self.places = [own], [(0, 0, own.shape[0])]

    def launch(self):
        self.hop += 1
        rows, half = self.own.shape[0], middle_row(self.own.shape[0])
        ahead, behind, t = self.ahead, self.behind, self.hop
        if t < self.last:
            self.places += [(self.ring.count - t, 0, rows), (t, 0, rows)]
        else:
            ahead, behind = ahead[:half], behind[half:]
            self.places += [(t, 0, half), (t, half, rows - half)]
        self.ahead, self.behind = self.ring.send(ahead, 1), self.ring.send(behind, -1)

    def land(self):
        self.ahead, self.behind = self.ring.order.land(self.ahead, self.behind)
        self.pieces += [self.ahead, self.behind]

    def rest(self):
        self.land()
        while self.hop < self.last - 1:
            self.launch()
            self.land()

    def collect(self, cuts=None):
        cuts = cuts or [(0, self.own.shape[0])]
        self.pieces[-1] = self.ring.order.tie(self.pieces[-1])
        return self.ring.order.mark(collect(self.pieces, self.ring.slots, self.places, cuts))


class Scatter:
    def __init__(self, ring, parts):
        self.ring, self.parts, self.hop = ring, parts, 0
        self.last = ring.count // 2
        self.came = None

    def kernel_call(self, offsets, body, came, outs, name):
        ring, parts = self.ring, self.parts
        count = ring.count

        def pick(part, offset):
            return pl.BlockSpec(
                (1,) + part.shape[1:], lambda i, slots: (slots[offset % count], 0, 0)
            )

        arrays, specs = [], []
        for part in parts:
            for offset in offsets:
                arrays.append(part)
                specs.append(pick(part, offset))
        for array in came:
            arrays.append(array)
            specs.append(pl.BlockSpec(array.shape, lambda i, slots: (0, 0)))
        return pl.pallas_call(
            lambda slots_ref, *refs: body(refs),
            grid_spec=pltpu.PrefetchScalarGridSpec(
                num_scalar_prefetch=1,
                grid=(1,),
                in_specs=specs,
                out_specs=[pl.BlockSpec(o, lambda i, slots: (0, 0)) for o in outs],
            ),
            out_shape=[jax.ShapeDtypeStruct(o, BF16) for o in outs],
            cost_estimate=SMALL,
            name=name,
        )(ring.slots, *arrays)

    def launch(self):
        self.hop += 1
        order, parts, n = self.ring.order, self.parts, len(self.parts)
        t = self.last + 1 - self.hop
        tops = [middle_row(p.shape[1]) for p in parts]
        if self.hop == 1:
            parts = order.tie(*parts)
            self.parts = parts = list(parts) if n > 1 else [parts]

            def first(refs):
                for p in range(n):
                    refs[n + 2 * p][...] = refs[p][0, : tops[p]]
                    refs[n + 2 * p + 1][...] = refs[p][0, tops[p] :]

            outs = []
            for p, part in enumerate(parts):
                outs += [(tops[p], part.shape[2]), (part.shape[1] - tops[p], part.shape[2])]
            send = self.kernel_call([t], first, [], outs, "scatter_first")
        else:

            def middle(refs):
                came, outs = refs[2 * n : 4 * n], refs[4 * n :]
                for p in range(n):
                    for way in range(2):
                        local, got = refs[2 * p + way], came[2 * p + way]
                        rows = slice(0, local.shape[1])
                        if self.hop == 2:
                            rows = slice(0, tops[p]) if way == 0 else slice(tops[p], rows.stop)
                            outs[2 * p + way][...] = local[0]
                        outs[2 * p + way][rows, :] = (
                            local[0, rows].astype(F32) + got[...].astype(F32)
                        ).astype(BF16)

            outs = []
            for part in parts:
                outs += [part.shape[1:]] * 2
            self.came[0] = order.tie(self.came[0])
            send = self.kernel_call([t, -t], middle, self.came, outs, "scatter_add")
        order.mark(send)
        self.came = [self.ring.send(array, 1 - 2 * (i % 2)) for i, array in enumerate(send)]

    def land(self):
        self.came = list(self.ring.order.land(*self.came))

    def rest(self):
        self.land()
        while self.hop < self.last:
            self.launch()
            self.land()

    def total(self):
        n = len(self.parts)

        def body(refs):
            for p in range(n):
                near = refs[n + 2 * p][...].astype(F32) + refs[n + 2 * p + 1][...].astype(F32)
                refs[3 * n + p][...] = (refs[p][0].astype(F32) + near).astype(BF16)

        outs = [part.shape[1:] for part in self.parts]
        self.came[0] = self.ring.order.tie(self.came[0])
        return self.ring.order.mark(self.kernel_call([0], body, self.came, outs, "scatter_sum"))


def per_device(
    latent,
    embed,
    seg_ids,
    positions,
    adapter_weight,
    query_weight,
    key_weight,
    value_weight,
    out_weight,
    gate_weight,
    up_weight,
    down_weight,
    gain_one,
    gain_two,
    gain_three,
    gain_four,
    cotangent,
):
    member = lax.axis_index("seq")
    count = lax.axis_size("fsdp")
    order = Order()
    ring = Ring(count, order)
    tokens, width = latent.shape[1], latent.shape[2]
    length = tokens * 4
    quarter = width // 4
    rows = query_weight.shape[0]
    adapter_rows = adapter_weight.shape[0]
    hidden_rows = down_weight.shape[0] // 4
    hidden_width = hidden_rows * count
    two = 2 * tokens

    def stack(*pieces):
        return jnp.concatenate(pieces, axis=0)

    def shares(part):
        return part.reshape(count, part.shape[0] // count, part.shape[1])

    def low(array):
        return array.astype(BF16)

    def high(array):
        return array.astype(F32)

    who = jnp.full((1,), member, jnp.int32)

    first_own, second_own = prepare(
        who,
        adapter_weight,
        (query_weight, key_weight, value_weight, out_weight),
        (gain_one, gain_two, gain_three, gain_four),
    )
    order.mark(first_own)
    joined = jnp.concatenate([latent[0], embed[0]], axis=1)
    order.mark(joined)
    adapters = Gather(ring, first_own)
    adapters.launch()
    across, beside = order.flip(joined, 2), order.flip(joined, 1)

    gate_up_own = order.mark(take_hidden(*order.tie(gate_weight, up_weight), who, count))
    down_own = lax.dynamic_slice_in_dim(
        order.tie(down_weight), member * hidden_rows, hidden_rows, 0
    )
    order.mark(down_own)
    qkvo = Gather(ring, second_own)
    gate_up, down = Gather(ring, gate_up_own), Gather(ring, down_own)

    def hop(*rings):
        for r in rings:
            r.land()
        for r in rings:
            r.launch()

    adapters.land()
    adapters.launch()
    segments = order.tie(seg_ids)[0]
    starts = jnp.sum((segments[None, :] < segments[:, None]).astype(jnp.int32), axis=1)
    places = (jnp.arange(length, dtype=jnp.int32) - starts).astype(F32)
    info = jnp.concatenate([who, starts[::BLOCK] // BLOCK])
    lane = np.arange(128) % HD
    frequency = ROPE_BASE ** (-2.0 * jnp.asarray(lane % (HD // 2), F32) / HD)
    angles = places[:, None] * frequency[None, :]
    cosine = jnp.cos(angles)
    sine = jnp.sin(angles) * jnp.asarray(np.where(lane < HD // 2, -1.0, 1.0), F32)
    seg_row = segments.reshape(length // BLOCK, 1, BLOCK)
    seg_col = jnp.broadcast_to(segments[:, None], (length, 128))
    cosine, sine, seg_col, seg_row, info = order.land(cosine, sine, seg_col, seg_row, info)
    hop(adapters)
    adapters.rest()
    adapters.launch()
    qkvo.launch()
    beside = order.land(beside)
    adapters.land()
    adapter_cols, gains = adapters.collect([(0, adapter_rows), (adapter_rows, adapter_rows + 8)])
    adapter_cols = adapter_cols.reshape(2 * width, quarter)
    gain_a, gain_b, gain_c, gain_d = [
        high(gains[:, g, :rows].reshape(1, width)) for g in range(4)
    ]
    hop(qkvo)
    stream_near = order.mark(stream_rows([order.tie(joined), beside], adapter_cols))
    across = order.land(across)
    diagonal = order.land(order.flip(across, 1))
    stream_far = order.mark(stream_rows([across, diagonal], adapter_cols))
    stream_cols = order.mark(stack(stream_near, stream_far))
    qkvo.land()
    stream_across, stream_beside = order.flip(stream_cols, 2), order.flip(stream_cols, 1)
    qkvo.launch()
    qkvo.rest()
    qkvo.launch()
    stream_beside, stream_across = order.land(stream_beside, stream_across)
    qkvo.land()
    stream_diagonal = order.flip(stream_across, 1)
    gate_up.launch()
    down.launch()
    qkvo_full = qkvo.collect()[0]
    stream_diagonal = order.land(stream_diagonal)

    out_sent = split_rows(order.tie(qkvo_full).reshape(width, width), who, 3 * quarter, width)
    order.mark(out_sent)
    out_came = order.swap(out_sent)
    normed_one, q_rows, k_rows, v_rows, stream = norm_qkv(
        [stream_cols, stream_beside, stream_across, stream_diagonal],
        gain_a,
        order.tie(qkvo_full),
        cosine,
        sine,
        who,
    )
    order.mark(q_rows)
    hop(gate_up, down)
    out_came = order.land(*out_came)
    out_rows = order.mark(assemble_cols([out_sent[0], *out_came], who, 1, BF16)[0])
    attended, lse = attend_forward(order.tie(q_rows), k_rows, v_rows, seg_row, seg_col, info)
    order.mark(attended)
    hop(gate_up, down)

    def weights_here():
        gate_up.land()
        down.land()
        wide, tall = gate_up.collect()[0], down.collect()[0]
        kept["hidden"] = wide.reshape(width, 2 * hidden_width), tall.reshape(hidden_width, width)

    kept = {}

    def scatter_seq(make, fill=None):
        far = order.mark(make(1))
        diagonal = order.land(order.flip(low(far[tokens:]), 1))
        crossing = order.mark(low(far[:tokens] + high(diagonal)))
        crossing = order.flip(crossing, 2)
        near = order.mark(make(0))
        beside = order.flip(low(near[tokens:]), 1)
        if fill is not None:
            fill()
        beside, crossing = order.land(beside, crossing)
        return near, beside, crossing

    branch = scatter_seq(
        lambda n: dot_nn(order.tie(attended)[n * two : (n + 1) * two], out_rows),
        lambda: hop(gate_up, down),
    )
    resid_one, middle, normed_own = rows_call(
        after_branch, branch, [stream], [gain_b, gain_c], ["wide", "wide", "low"], "after_branch"
    )(who)
    order.mark(normed_own)

    def gather_seq(own, fill=None, near=None):
        across, beside = order.flip(own, 2), order.flip(own, 1)
        beside = order.land(beside)
        close = order.mark(stack(own, beside))
        if fill is not None:
            fill()
        done = near(close) if near is not None else None
        across = order.land(across)
        diagonal = order.land(order.flip(across, 1))
        return close, order.mark(stack(across, diagonal)), done

    gate_act, up_act, hidden = [], [], []

    def into_hidden(rows_in):
        act = dot_nn(order.tie(rows_in), kept["hidden"][0])
        gate_act.append(act[:, :hidden_width])
        up_act.append(act[:, hidden_width:])
        hidden.append(low(gate_act[-1] / (1.0 + jnp.exp(-gate_act[-1])) * up_act[-1]))
        order.mark(hidden[-1])
        return order.mark(dot_nn(hidden[-1], kept["hidden"][1]))

    normed_near, normed_far, mlp_near = gather_seq(normed_own, weights_here, into_hidden)
    gate_up_full, down_full = kept["hidden"]
    mlp_far = into_hidden(normed_far)
    mlp = scatter_seq(lambda n: (mlp_near, mlp_far)[n])
    d_resid_two, d_mlp_own, result, gain_four_part = rows_call(
        after_mlp,
        mlp,
        [middle, cotangent[0]],
        [gain_d],
        ["wide", "low", "low", "sum"],
        "after_mlp",
    )(who)
    order.mark(d_mlp_own)

    def through_hidden(n, d_mlp):
        d_hidden = dot_nt(order.tie(d_mlp), down_full)
        gate, sigmoid = gate_act[n], 1.0 / (1.0 + jnp.exp(-gate_act[n]))
        d_gate = low(d_hidden * up_act[n] * sigmoid * (1.0 + gate * (1.0 - sigmoid)))
        d_up = low(d_hidden * (gate * sigmoid))
        return order.mark(jnp.concatenate([d_gate, d_up], axis=1))

    d_near, d_far, d_gate_up_near = gather_seq(
        d_mlp_own, None, lambda d_mlp: through_hidden(0, d_mlp)
    )
    d_gate_up = [d_gate_up_near, through_hidden(1, d_far)]
    rings = {}

    def hidden_grads():
        parts = hidden_terms(
            [order.tie(normed_near), normed_far], d_gate_up, hidden, [d_near, d_far], count
        )
        order.mark(parts)
        kept["hidden_sum"] = lax.psum_scatter(parts, "fsdp", scatter_dimension=0)

    d_normed_three = scatter_seq(
        lambda n: dot_nt(order.tie(d_gate_up[n]), gate_up_full), hidden_grads
    )
    d_resid_one, d_branch_own, gain_three_part, gain_two_part = rows_call(
        after_hidden,
        d_normed_three,
        [middle, resid_one, d_resid_two],
        [gain_b, gain_c],
        ["wide", "low", "sum", "sum"],
        "after_hidden",
    )(who)
    order.mark(d_branch_own)

    def into_attended(n, d_branch):
        grads = order.mark(low(dot_nt(order.tie(d_branch), out_rows)))
        return grads, order.mark(dot_tn(order.tie(attended)[n * two : (n + 1) * two], d_branch))

    _, d_branch_far, near_terms = gather_seq(
        d_branch_own, None, lambda d_branch: into_attended(0, d_branch)
    )
    adapter_across, adapter_beside = order.flip(adapter_cols, 2), order.flip(adapter_cols, 1)
    far_terms = into_attended(1, d_branch_far)
    d_attended = order.mark(stack(near_terms[0], far_terms[0]))
    out_part = order.mark(low(near_terms[1] + far_terms[1]))
    out_split = split_cols(order.tie(out_part), who)
    order.mark(out_split)
    out_sums = order.swap(out_split)
    d_qkv = attend_backward(
        q_rows,
        k_rows,
        v_rows,
        order.tie(d_attended),
        attended,
        lse,
        cosine,
        sine,
        seg_row,
        seg_col,
        info,
    )
    order.mark(d_qkv)
    qkv_cols = qkvo_full.reshape(width, width)[:, : 3 * quarter]

    def qkv_grads():
        sums = order.land(*out_sums)
        out_terms = assemble_rows([out_split[0], *sums], who, BF16)
        order.mark(out_terms)
        qkv_part = order.mark(low(dot_tn(order.tie(normed_one), d_qkv)))
        both = jnp.concatenate([shares(qkv_part), shares(out_terms)], axis=2)
        order.mark(both)
        kept["diagonal"] = order.flip(kept["across"], 1)
        rings["qkvo"] = Scatter(ring, [both])
        rings["qkvo"].launch()

    def into_normed(n):
        terms = dot_nt(order.tie(d_qkv)[n * two : (n + 1) * two], qkv_cols)
        if n == 1:
            order.mark(terms)
            kept["across"], kept["beside"] = order.land(adapter_across, adapter_beside)
            terms = order.tie(terms)
        return terms

    d_normed_one = scatter_seq(into_normed, qkv_grads)
    *d_split, gain_one_part = rows_call(
        after_attention,
        d_normed_one,
        [stream, d_resid_one],
        [gain_a],
        ["split"] * 4 + ["sum"],
        "after_attention",
    )(who)
    order.mark(d_split)
    d_cols = order.swap(d_split)
    hop(rings["qkvo"])
    d_cols = [d_split[0], *order.land(*d_cols)]
    hop(rings["qkvo"])
    adapter_part = adapter_terms(
        [order.tie(joined), beside, across, diagonal],
        d_cols,
        [gain_one_part, gain_two_part, gain_three_part, gain_four_part],
        count,
    )
    order.mark(adapter_part)
    rings["adapter"] = Scatter(ring, [adapter_part])
    rings["adapter"].launch()

    def exchange(total):
        return total, order.flip(total, 1), order.flip(total, 2)

    def settle(pieces):
        beside, across = order.land(*pieces[1:])
        return [pieces[0], beside, across, order.flip(across, 1)]

    hop(rings["qkvo"])
    kept["hidden_sum"] = order.land(kept["hidden_sum"])
    kept["hidden_grads"] = lax.all_gather(kept["hidden_sum"], "seq")
    adapter_diagonal = order.land(kept["diagonal"])
    latent_grad, embed_grad = joined_back(
        order.tie(d_split[0]),
        d_split[1:],
        [adapter_cols, kept["beside"], kept["across"], adapter_diagonal],
    )
    order.mark(latent_grad)
    hop(rings["adapter"])
    rings["qkvo"].rest()
    qkvo_done = exchange(rings["qkvo"].total()[0])
    hop(rings["adapter"])
    qkvo_done = settle(qkvo_done)
    hop(rings["adapter"])
    gate_grad, up_grad, down_grad = restore_hidden(
        order.land(kept["hidden_grads"]), rows, 2 * hidden_width, hidden_rows, width, count
    )
    order.mark(gate_grad)
    rings["adapter"].rest()
    last_done = exchange(rings["adapter"].total()[0])
    qkvo_done[3] = order.land(qkvo_done[3])
    query_grad, key_grad, value_grad, out_grad = assemble_cols(
        [order.tie(qkvo_done[0]), *qkvo_done[1:]], who, 4, F32
    )
    order.mark(query_grad)
    last_done = settle(last_done)
    last_done[3] = order.land(last_done[3])
    adapter_grad, *gain_grads = assemble_last(last_done, who, adapter_rows, rows)
    return (
        result[None],
        latent_grad[None],
        embed_grad[None],
        adapter_grad,
        query_grad,
        key_grad,
        value_grad,
        out_grad,
        gate_grad,
        up_grad,
        down_grad,
        gain_grads[0][0],
        gain_grads[1][0],
        gain_grads[2][0],
        gain_grads[3][0],
    )


def solution(mesh):
    rows, vector = P("fsdp", None), P("fsdp")
    tokens = P("fsdp", "seq", None)
    placed = (tokens, tokens, rows, P("fsdp", "seq")) + (rows,) * 8 + (vector,) * 4 + (tokens,)
    return jax.shard_map(
        per_device,
        mesh=mesh,
        in_specs=placed,
        out_specs=(tokens,) * 3 + (rows,) * 8 + (vector,) * 4,
        check_vma=False,
    )
```

```python
import jax
import jax.numpy as jnp
import numpy as np
from jax import lax
from jax.experimental import pallas as pl
from jax.experimental.pallas import tpu as pltpu
from jax.sharding import PartitionSpec as P

H = 16
HD = 64
EPSILON = 1e-06
ROPE_BASE = 50000.0
NEG_FILL = -1e30
BLOCK = 256
F32 = jnp.float32
SMALL = pl.CostEstimate(flops=1, bytes_accessed=1, transcendentals=0)
LONG = pl.CostEstimate(flops=10**11, bytes_accessed=1, transcendentals=0)
BF16 = jnp.bfloat16


def dot_nn(left, right):
    return lax.dot_general(left, right, (((1,), (0,)), ((), ())), preferred_element_type=F32)


def dot_tn(left, right):
    return lax.dot_general(left, right, (((0,), (0,)), ((), ())), preferred_element_type=F32)


def dot_nt(left, right):
    return lax.dot_general(left, right, (((1,), (1,)), ((), ())), preferred_element_type=F32)


def inverse_root(values):
    return lax.rsqrt(jnp.mean(values * values, axis=-1, keepdims=True) + EPSILON)


def norm_back(values, root, upstream):
    inner_mean = jnp.mean(upstream * values, axis=-1, keepdims=True)
    return root * upstream - values * root * root * root * inner_mean


def swap_halves(values):
    lane = lax.broadcasted_iota(jnp.int32, values.shape, 1)
    width = values.shape[1]
    ahead = pltpu.roll(values, width - HD // 2, 1)
    behind = pltpu.roll(values, HD // 2, 1)
    return jnp.where(lane % HD < HD // 2, ahead, behind)


def stack_heads(rows):
    lane = lax.broadcasted_iota(jnp.int32, rows.shape, 1)
    zero = jnp.zeros_like(rows)
    count = rows.shape[1] // HD
    return jnp.concatenate([jnp.where(lane // HD == h, rows, zero) for h in range(count)], axis=0)


def allowed_block(key_segs, query_segs, key_begin, query_begin, count):
    rows, cols = key_segs.shape[0], query_segs.shape[1]
    key_index = key_begin + lax.broadcasted_iota(jnp.int32, (rows, cols), 0)
    query_index = query_begin + lax.broadcasted_iota(jnp.int32, (rows, cols), 1)
    keep = (key_segs == query_segs) & (key_index <= query_index)
    bias = jnp.where(keep, 0.0, NEG_FILL)
    return jnp.concatenate([bias] * count, axis=1)


def forward_kernel(
    info_ref, q_ref, k_ref, v_ref, segq_ref, segk_ref, out_ref, lse_ref, score_ref, acc_ref
):
    i = pl.program_id(0)
    member = info_ref[0]
    heads = q_ref.shape[1] // HD
    stacked = stack_heads(q_ref[...] * jnp.asarray(HD ** (-0.5), BF16))
    begin = info_ref[1 + i]
    wide = heads * BLOCK

    def score_step(j, high):
        base = pl.multiple_of(j * BLOCK, BLOCK)
        keys = k_ref[pl.ds(pl.multiple_of((j ^ member) * BLOCK, BLOCK), BLOCK), :]
        scores = dot_nt(keys, stacked)
        scores = scores + allowed_block(
            segk_ref[pl.ds(base, BLOCK), :1], segq_ref[0], base, i * BLOCK, heads
        )
        score_ref[pl.ds(base, BLOCK), :] = scores
        return jnp.maximum(high, jnp.max(scores, axis=0, keepdims=True))

    high = lax.fori_loop(begin, i + 1, score_step, jnp.full((1, wide), NEG_FILL, F32))
    acc_ref[...] = jnp.zeros_like(acc_ref)

    def value_step(j, total):
        base = pl.multiple_of(j * BLOCK, BLOCK)
        expos = jnp.exp(score_ref[pl.ds(base, BLOCK), :] - high)
        values = v_ref[pl.ds(pl.multiple_of((j ^ member) * BLOCK, BLOCK), BLOCK), :]
        acc_ref[...] += dot_tn(values, expos.astype(BF16))
        return total + jnp.sum(expos, axis=0, keepdims=True)

    total = lax.fori_loop(begin, i + 1, value_step, jnp.zeros((1, wide), F32))
    scaled = acc_ref[...] / total
    pieces = [scaled[h * HD : (h + 1) * HD, h * BLOCK : (h + 1) * BLOCK] for h in range(heads)]
    out_ref[...] = jnp.transpose(jnp.concatenate(pieces, axis=0), (1, 0)).astype(BF16)
    lse_ref[0] = high + jnp.log(total)


def attend_forward(q, k, v, seg_row, seg_col, info):
    length, width = q.shape
    heads = width // HD
    blocks = length // BLOCK
    part = pl.BlockSpec((BLOCK, width), lambda i, info: (i ^ info[0], 0))
    whole = pl.BlockSpec((length, width), lambda i, info: (0, 0))
    return pl.pallas_call(
        forward_kernel,
        grid_spec=pltpu.PrefetchScalarGridSpec(
            num_scalar_prefetch=1,
            grid=(blocks,),
            in_specs=[
                part,
                whole,
                whole,
                pl.BlockSpec((1, 1, BLOCK), lambda i, info: (i, 0, 0)),
                pl.BlockSpec((length, 128), lambda i, info: (0, 0)),
            ],
            out_specs=[part, pl.BlockSpec((1, 1, heads * BLOCK), lambda i, info: (i, 0, 0))],
            scratch_shapes=[
                pltpu.VMEM((length, heads * BLOCK), F32),
                pltpu.VMEM((width, heads * BLOCK), F32),
            ],
        ),
        out_shape=[
            jax.ShapeDtypeStruct((length, width), BF16),
            jax.ShapeDtypeStruct((blocks, 1, heads * BLOCK), F32),
        ],
        cost_estimate=SMALL,
        name="attend_forward",
    )(info, q, k, v, seg_row, seg_col)


def backward_kernel(
    info_ref,
    q_ref,
    k_ref,
    v_ref,
    grad_ref,
    out_ref,
    lse_ref,
    cos_ref,
    sin_ref,
    segq_ref,
    segk_ref,
    d_ref,
    dk_acc,
    dv_acc,
    dq_acc,
):
    i = pl.program_id(0)
    member = info_ref[0]
    width = q_ref.shape[1]
    heads = width // HD
    factor = HD ** (-0.5)

    @pl.when(i == 0)
    def _():
        dk_acc[...] = jnp.zeros_like(dk_acc)
        dv_acc[...] = jnp.zeros_like(dv_acc)

    stacked = stack_heads(q_ref[...] * jnp.asarray(factor, BF16))
    grads = grad_ref[...]
    grad_stacked = stack_heads(grads)
    product = jnp.transpose(grads.astype(F32) * out_ref[...].astype(F32), (1, 0))
    inner = jnp.concatenate(
        [
            jnp.sum(product[h * HD : (h + 1) * HD, :], axis=0, keepdims=True)
            for h in range(heads)
        ],
        axis=1,
    )
    log_sum = lse_ref[0]
    dq_acc[...] = jnp.zeros_like(dq_acc)

    def step(j, carry):
        base = pl.multiple_of(j * BLOCK, BLOCK)
        here = pl.multiple_of((j ^ member) * BLOCK, BLOCK)
        keys = k_ref[pl.ds(here, BLOCK), :]
        values = v_ref[pl.ds(here, BLOCK), :]
        scores = dot_nt(keys, stacked)
        scores = scores + allowed_block(
            segk_ref[pl.ds(base, BLOCK), :1], segq_ref[0], base, i * BLOCK, heads
        )
        probs = jnp.exp(scores - log_sum)
        dv_acc[pl.ds(base, BLOCK), :] += dot_nn(probs.astype(BF16), grad_stacked)
        grad_probs = dot_nt(values, grad_stacked)
        grad_scores = (probs * (grad_probs - inner)).astype(BF16)
        dk_acc[pl.ds(base, BLOCK), :] += dot_nn(grad_scores, stacked)
        dq_acc[...] += dot_tn(keys, grad_scores)
        return carry

    lax.fori_loop(info_ref[1 + i], i + 1, step, 0)

    def unrotate(values, base):
        values = values.astype(BF16).astype(F32)
        cosine = jnp.concatenate([cos_ref[pl.ds(base, BLOCK), :]] * (width // 128), axis=1)
        sine = jnp.concatenate([sin_ref[pl.ds(base, BLOCK), :]] * (width // 128), axis=1)
        return (values * cosine - swap_halves(values) * sine).astype(BF16)

    pieces = [dq_acc[h * HD : (h + 1) * HD, h * BLOCK : (h + 1) * BLOCK] for h in range(heads)]
    dq = jnp.transpose(jnp.concatenate(pieces, axis=0), (1, 0)) * factor
    here = pl.multiple_of((i ^ member) * BLOCK, BLOCK)
    d_ref[pl.ds(here, BLOCK), :width] = unrotate(dq, pl.multiple_of(i * BLOCK, BLOCK))

    @pl.when(i == pl.num_programs(0) - 1)
    def _():
        for j in range(k_ref.shape[0] // BLOCK):
            there = pl.multiple_of((j ^ member) * BLOCK, BLOCK)
            rows = slice(j * BLOCK, (j + 1) * BLOCK)
            d_ref[pl.ds(there, BLOCK), width : 2 * width] = unrotate(dk_acc[rows, :], j * BLOCK)
            d_ref[pl.ds(there, BLOCK), 2 * width :] = dv_acc[rows, :].astype(BF16)


def attend_backward(q, k, v, grads, outs, lse, cosine, sine, seg_row, seg_col, info):
    length, width = q.shape
    heads = width // HD
    blocks = length // BLOCK
    part = pl.BlockSpec((BLOCK, width), lambda i, info: (i ^ info[0], 0))
    whole = pl.BlockSpec((length, width), lambda i, info: (0, 0))
    return pl.pallas_call(
        backward_kernel,
        grid_spec=pltpu.PrefetchScalarGridSpec(
            num_scalar_prefetch=1,
            grid=(blocks,),
            in_specs=[
                part,
                whole,
                whole,
                part,
                part,
                pl.BlockSpec((1, 1, heads * BLOCK), lambda i, info: (i, 0, 0)),
                pl.BlockSpec((length, 128), lambda i, info: (0, 0)),
                pl.BlockSpec((length, 128), lambda i, info: (0, 0)),
                pl.BlockSpec((1, 1, BLOCK), lambda i, info: (i, 0, 0)),
                pl.BlockSpec((length, 128), lambda i, info: (0, 0)),
            ],
            out_specs=pl.BlockSpec((length, 3 * width), lambda i, info: (0, 0)),
            scratch_shapes=[
                pltpu.VMEM((length, width), F32),
                pltpu.VMEM((length, width), F32),
                pltpu.VMEM((width, heads * BLOCK), F32),
            ],
        ),
        out_shape=jax.ShapeDtypeStruct((length, 3 * width), BF16),
        cost_estimate=SMALL,
        name="attend_backward",
    )(info, q, k, v, grads, outs, lse, cosine, sine, seg_row, seg_col)


def choose(refs, want, rows=None, cols=None):
    rows = slice(None) if rows is None else rows
    cols = slice(None) if cols is None else cols
    value = refs[0][rows, cols]
    for k in range(1, len(refs)):
        value = jnp.where(want == k, refs[k][rows, cols], value)
    return value


def small_call(kernel, info, arrays, out_shapes, name):
    return pl.pallas_call(
        kernel,
        grid_spec=pltpu.PrefetchScalarGridSpec(
            num_scalar_prefetch=1,
            grid=(1,),
            in_specs=[
                pl.BlockSpec(a.shape, lambda i, info, n=a.ndim: (0,) * n) for a in arrays
            ],
            out_specs=[
                pl.BlockSpec(o.shape, lambda i, info, n=len(o.shape): (0,) * n)
                for o in out_shapes
            ],
        ),
        out_shape=out_shapes,
        cost_estimate=SMALL,
        name=name,
    )(info, *arrays)


def assemble_cols(pieces, info, groups, dtype):
    rows, w = pieces[0].shape[0], pieces[0].shape[1] // groups

    def kernel(info_ref, *refs):
        for g in range(groups):
            for m in range(4):
                value = choose(refs[:4], info_ref[0] ^ m, cols=slice(g * w, (g + 1) * w))
                refs[4 + g][:, m * w : (m + 1) * w] = value.astype(dtype)

    shapes = [jax.ShapeDtypeStruct((rows, 4 * w), dtype) for _ in range(groups)]
    return small_call(kernel, info, pieces, shapes, "assemble_cols")


def assemble_rows(pieces, info, dtype):
    rows, w = pieces[0].shape

    def kernel(info_ref, *refs):
        for m in range(4):
            refs[4][m * rows : (m + 1) * rows, :] = choose(refs[:4], info_ref[0] ^ m).astype(dtype)

    return small_call(
        kernel, info, pieces, [jax.ShapeDtypeStruct((4 * rows, w), dtype)], "assemble_rows"
    )[0]


def split_cols(array, info):
    rows, w = array.shape[0], array.shape[1] // 4

    def kernel(info_ref, ref, *outs):
        for k in range(4):
            value = ref[:, :w]
            for m in range(1, 4):
                value = jnp.where((info_ref[0] ^ k) == m, ref[:, m * w : (m + 1) * w], value)
            outs[k][...] = value

    shapes = [jax.ShapeDtypeStruct((rows, w), array.dtype) for _ in range(4)]
    return small_call(kernel, info, [array], shapes, "split_cols")


def split_rows(array, info, low, high):
    rows = array.shape[0] // 4

    def kernel(info_ref, ref, *outs):
        for k in range(4):
            start = pl.multiple_of((info_ref[0] ^ k) * rows, rows)
            outs[k][...] = ref[pl.ds(start, rows), low:high]

    shapes = [jax.ShapeDtypeStruct((rows, high - low), array.dtype) for _ in range(4)]
    return small_call(kernel, info, [array], shapes, "split_rows")


def collect(pieces, slots, places, cuts):
    cols, count = pieces[0].shape[1], slots.shape[0]

    def kernel(slot_ref, *refs):
        ins, outs = refs[: len(pieces)], refs[len(pieces) :]
        for ref, (p, row, size) in zip(ins, places):
            for out, (low, high) in zip(outs, cuts):
                begin, end = max(low, row), min(high, row + size)
                if begin < end:
                    out[slot_ref[p], begin - low : end - low, :] = ref[begin - row : end - row, :]

    shapes = [jax.ShapeDtypeStruct((count, high - low, cols), pieces[0].dtype) for low, high in cuts]
    return small_call(kernel, slots, pieces, shapes, "collect")


def hidden_plan(rows, both, hidden_rows, width):
    step = -(-hidden_rows // 16) * 16
    base = both // 128 * rows
    return base, step, base + width // 128 * step


def take_hidden(gate, up, info, count):
    rows, full = gate.shape
    w = full // count // 4

    def kernel(info_ref, gate_ref, up_ref, out_ref):
        for m in range(4):

            @pl.when(info_ref[0] == m)
            def _(m=m):
                for n, ref in enumerate((gate_ref, up_ref)):
                    for f in range(count):
                        at, low = (n * count + f) * w, (4 * f + m) * w
                        out_ref[:, at : at + w] = ref[:, low : low + w]

    shape = jax.ShapeDtypeStruct((rows, full // 2), gate.dtype)
    return small_call(kernel, info, [gate, up], [shape], "take_hidden")[0]


def restore_hidden(packed, rows, both, hidden_rows, width, count):
    total = packed.shape[1]
    base, step, _ = hidden_plan(rows, both, hidden_rows, width)
    w = both // 2 // count

    def kernel(ref, gate_ref, up_ref, down_ref):
        for m in range(4):
            tiles = [ref[m, c * rows : (c + 1) * rows, :] for c in range(both // 128)]
            value = jnp.concatenate(tiles, axis=1).astype(F32)
            for n, out in enumerate((gate_ref, up_ref)):
                for f in range(count):
                    at, low = (n * count + f) * w, (4 * f + m) * w
                    out[:, low : low + w] = value[:, at : at + w]
            for c in range(width // 128):
                at = base + c * step
                part = ref[m, at : at + hidden_rows, :].astype(F32)
                down_ref[m * hidden_rows : (m + 1) * hidden_rows, c * 128 : (c + 1) * 128] = part

    outs = [(rows, 2 * both), (rows, 2 * both), (4 * hidden_rows, width)]
    return pl.pallas_call(
        kernel,
        grid=(1,),
        in_specs=[pl.BlockSpec((4, total, 128), lambda i: (0, 0, 0))],
        out_specs=[pl.BlockSpec(o, lambda i: (0, 0)) for o in outs],
        out_shape=[jax.ShapeDtypeStruct(o, F32) for o in outs],
        cost_estimate=SMALL,
        name="restore_hidden",
    )(packed)


def prepare_kernel(info_ref, adapter_ref, q_ref, k_ref, v_ref, o_ref, *refs):
    gains, first_ref, second_ref = refs[:4], refs[4], refs[5]
    rows, quarter = adapter_ref.shape
    first_ref[:rows, :] = adapter_ref[...]
    first_ref[rows:, :] = jnp.zeros((first_ref.shape[0] - rows, quarter), BF16)
    size = gains[0].shape[1]
    for g in range(4):
        first_ref[rows + g : rows + g + 1, :size] = gains[g][...]
    for n, ref in enumerate((q_ref, k_ref, v_ref, o_ref)):
        second_ref[:, n * quarter : (n + 1) * quarter] = ref[...]


def prepare(info, adapter, weights, gains):
    quarter = adapter.shape[1] // 4
    rows = weights[0].shape[0]
    own = lambda i, info: (0, info[0])
    return pl.pallas_call(
        prepare_kernel,
        grid_spec=pltpu.PrefetchScalarGridSpec(
            num_scalar_prefetch=1,
            grid=(1,),
            in_specs=[pl.BlockSpec((adapter.shape[0], quarter), own)]
            + [pl.BlockSpec((rows, quarter), own) for _ in weights]
            + [pl.BlockSpec((1, rows), lambda i, info: (0, 0)) for _ in gains],
            out_specs=[
                pl.BlockSpec((adapter.shape[0] + 8, quarter), lambda i, info: (0, 0)),
                pl.BlockSpec((rows, 4 * quarter), lambda i, info: (0, 0)),
            ],
        ),
        out_shape=[
            jax.ShapeDtypeStruct((adapter.shape[0] + 8, quarter), BF16),
            jax.ShapeDtypeStruct((rows, 4 * quarter), BF16),
        ],
        cost_estimate=SMALL,
        name="prepare",
    )(info, adapter, *weights, *[g.reshape(1, -1) for g in gains])


def qkv_kernel(
    info_ref,
    p0_ref,
    p1_ref,
    p2_ref,
    p3_ref,
    gain_ref,
    weight_ref,
    cos_ref,
    sin_ref,
    normed_ref,
    q_ref,
    k_ref,
    v_ref,
    stream_ref,
):
    i = pl.program_id(0)
    member = info_ref[0]
    refs = (p0_ref, p1_ref, p2_ref, p3_ref)
    stream = jnp.concatenate([choose(refs, member ^ m).astype(F32) for m in range(4)], axis=1)

    @pl.when(i == 0)
    def _():
        stream_ref[...] = stream

    normed = (stream * inverse_root(stream) * gain_ref[...]).astype(BF16)
    normed_ref[...] = normed
    count, rows, width = weight_ref.shape
    weight = weight_ref[...].reshape(count * rows, width)
    product = dot_nn(normed, weight)
    quarter = width // 3
    cosine = jnp.concatenate([cos_ref[...]] * (quarter // 128), axis=1)
    sine = jnp.concatenate([sin_ref[...]] * (quarter // 128), axis=1)
    for n, ref in enumerate((q_ref, k_ref)):
        values = product[:, n * quarter : (n + 1) * quarter]
        ref[...] = (values * cosine + swap_halves(values) * sine).astype(BF16)
    v_ref[...] = product[:, 2 * quarter :].astype(BF16)


def norm_qkv(pieces, gain, weights, cosine, sine, info):
    length, quarter = pieces[0].shape
    count, rows, _ = weights.shape
    block = pl.BlockSpec((BLOCK, quarter), lambda i, info: (i, 0))
    natural = pl.BlockSpec((BLOCK, 128), lambda i, info: (i ^ info[0], 0))
    small = jax.ShapeDtypeStruct((length, quarter), BF16)
    return pl.pallas_call(
        qkv_kernel,
        grid_spec=pltpu.PrefetchScalarGridSpec(
            num_scalar_prefetch=1,
            grid=(length // BLOCK,),
            in_specs=[
                pl.BlockSpec((BLOCK, quarter), lambda i, info, k=k: (i ^ k, 0)) for k in range(4)
            ]
            + [
                pl.BlockSpec((1, 4 * quarter), lambda i, info: (0, 0)),
                pl.BlockSpec((count, rows, 3 * quarter), lambda i, info: (0, 0, 0)),
                natural,
                natural,
            ],
            out_specs=[
                pl.BlockSpec((BLOCK, 4 * quarter), lambda i, info: (i, 0)),
                block,
                block,
                block,
                pl.BlockSpec((BLOCK, 4 * quarter), lambda i, info: (0, 0)),
            ],
        ),
        out_shape=[
            jax.ShapeDtypeStruct((length, 4 * quarter), BF16),
            small,
            small,
            small,
            jax.ShapeDtypeStruct((BLOCK, 4 * quarter), F32),
        ],
        cost_estimate=SMALL,
        name="norm_qkv",
    )(info, *pieces, gain, weights, cosine, sine)


def assemble_last(pieces, info, cut, size):
    rows, w = pieces[0].shape

    def kernel(info_ref, *refs):
        for m in range(4):
            value = choose(refs[:4], info_ref[0] ^ m, rows=slice(0, cut))
            refs[4][:, m * w : (m + 1) * w] = value.astype(F32)
        total = sum(ref[cut:, :].astype(F32) for ref in refs[:4])
        for g in range(4):
            refs[5 + g][...] = total[g : g + 1, :size]

    shapes = [jax.ShapeDtypeStruct((cut, 4 * w), F32)]
    shapes += [jax.ShapeDtypeStruct((1, size), F32) for _ in range(4)]
    return small_call(kernel, info, pieces, shapes, "assemble_last")


def stream_rows(blocks, weight):
    tokens, quarter, n = blocks[0].shape[0], weight.shape[1], len(blocks)

    def kernel(*refs):
        for k in range(n):
            value = dot_nn(refs[k][...], refs[n][...])
            refs[n + 1][k * tokens : (k + 1) * tokens, :] = value.astype(BF16)

    return pl.pallas_call(
        kernel,
        out_shape=jax.ShapeDtypeStruct((n * tokens, quarter), BF16),
        cost_estimate=SMALL,
        name="stream_rows",
    )(*blocks, weight)


def adapter_terms(blocks, d_cols, gains, count):
    width, quarter, n = blocks[0].shape[1] // 2, d_cols[0].shape[1], len(blocks)
    rows, size = 2 * width // count, width // count

    def kernel(*refs):
        gain_refs, out_ref = refs[2 * n : 2 * n + 4], refs[2 * n + 4]
        out_ref[:, rows:, :] = jnp.zeros((count, 8, quarter), BF16)
        for half in range(2):
            cols = slice(half * width, (half + 1) * width)
            total = dot_tn(refs[0][:, cols], refs[n][...])
            for k in range(1, n):
                total = total + dot_tn(refs[k][:, cols], refs[n + k][...])
            total = total.astype(BF16)
            for f in range(count // 2):
                out_ref[half * count // 2 + f, :rows, :] = total[f * rows : (f + 1) * rows, :]
        for g, ref in enumerate(gain_refs):
            for f in range(count):
                value = ref[:, f * size : (f + 1) * size].astype(BF16)
                out_ref[f, rows + g : rows + g + 1, :size] = value

    return pl.pallas_call(
        kernel,
        out_shape=jax.ShapeDtypeStruct((count, rows + 8, quarter), BF16),
        cost_estimate=SMALL,
        name="adapter_terms",
    )(*blocks, *d_cols, *gains)


def joined_back(first, others, weights):
    pieces = [first, *others]
    tokens, quarter = first.shape
    blocks = weights[0].shape[0] // 512

    def kernel(*refs):
        total = dot_nt(refs[0][...], refs[4][...])
        for k in range(1, 4):
            total = total + dot_nt(refs[k][...], refs[4 + k][...])
        i = pl.program_id(0)

        @pl.when(i < blocks // 2)
        def _():
            refs[8][...] = total

        @pl.when(i >= blocks // 2)
        def _():
            refs[9][...] = total

    half = blocks // 2
    return pl.pallas_call(
        kernel,
        grid=(blocks,),
        in_specs=[pl.BlockSpec((tokens, quarter), lambda i: (0, 0)) for _ in pieces]
        + [pl.BlockSpec((512, quarter), lambda i: (i, 0)) for _ in weights],
        out_specs=[
            pl.BlockSpec((tokens, 512), lambda i: (0, jnp.minimum(i, half - 1))),
            pl.BlockSpec((tokens, 512), lambda i: (0, jnp.maximum(i - half, 0))),
        ],
        out_shape=[jax.ShapeDtypeStruct((tokens, 512 * half), F32) for _ in range(2)],
        cost_estimate=SMALL,
        name="joined_back",
    )(*pieces, *weights)


def rows_call(body, sums, cols, gains, outs, name):
    near, beside, crossing = sums
    tokens, width = beside.shape
    step = tokens // 2
    n = 3 + len(cols) + len(gains)

    def kernel(info_ref, *refs):
        total = refs[0][...] + refs[1][...].astype(F32) + refs[2][...].astype(F32)
        values = [ref[...].astype(F32) for ref in refs[3 : 3 + len(cols)]]
        results = body(info_ref, total, *values, *[ref[...] for ref in refs[3 + len(cols) : n]])
        for ref, value in zip(refs[n:], results):
            if ref.shape[0] == 1:

                @pl.when(pl.program_id(0) == 0)
                def _(ref=ref):
                    ref[...] = jnp.zeros_like(ref)

                ref[...] += jnp.sum(value, axis=0, keepdims=True)
            else:
                ref[...] = value.astype(ref.dtype)

    def spec(cols):
        return pl.BlockSpec((step, cols), lambda i, info: (i, 0))

    fixed = pl.BlockSpec((1, width), lambda i, info: (0, 0))
    shapes, specs = [], []
    for kind in outs:
        wide = width if kind != "split" else width // 4
        if kind == "sum":
            shapes.append(jax.ShapeDtypeStruct((1, width), F32))
            specs.append(fixed)
        else:
            shapes.append(jax.ShapeDtypeStruct((tokens, wide), F32 if kind == "wide" else BF16))
            specs.append(spec(wide))

    def run(info):
        return pl.pallas_call(
            kernel,
            grid_spec=pltpu.PrefetchScalarGridSpec(
                num_scalar_prefetch=1,
                grid=(2,),
                in_specs=[spec(width)] * (3 + len(cols)) + [fixed] * len(gains),
                out_specs=specs,
            ),
            out_shape=shapes,
            cost_estimate=LONG if name == "after_hidden" else SMALL,
            name=name,
        )(info, near, beside, crossing, *cols, *gains)

    return run


def after_branch(info, total, stream, gain_b, gain_c):
    resid = total + stream
    middle = resid * inverse_root(resid) * gain_b
    return resid, middle, middle * inverse_root(middle) * gain_c


def after_mlp(info, total, middle, upstream, gain_d):
    resid = total + middle
    root = inverse_root(resid)
    d_resid = norm_back(resid, root, upstream * gain_d)
    scaled = resid * root
    return d_resid, d_resid, scaled * gain_d, upstream * scaled


def after_hidden(info, d_normed, middle, resid, d_resid_two, gain_b, gain_c):
    root_three, root_two = inverse_root(middle), inverse_root(resid)
    d_middle = d_resid_two + norm_back(middle, root_three, d_normed * gain_c)
    d_resid = norm_back(resid, root_two, d_middle * gain_b)
    return d_resid, d_resid, d_normed * middle * root_three, d_middle * resid * root_two


def after_attention(info, d_normed, stream, d_resid, gain_a):
    root = inverse_root(stream)
    d_stream = d_resid + norm_back(stream, root, d_normed * gain_a)
    w = d_stream.shape[1] // 4
    pieces = []
    for k in range(4):
        value = d_stream[:, :w]
        for m in range(1, 4):
            value = jnp.where((info[0] ^ k) == m, d_stream[:, m * w : (m + 1) * w], value)
        pieces.append(value)
    return (*pieces, d_normed * stream * root)


def hidden_terms(normed, d_acts, hidden, d_mlp, count):
    tokens, width = normed[0].shape
    rows, both, hidden_width = width // count, d_acts[0].shape[1], hidden[0].shape[1]
    hidden_rows = hidden_width // count
    base, step, total = hidden_plan(rows, both, hidden_rows, width)

    def kernel(n0, n1, d0, d1, h0, h1, m0, m1, out_ref):
        def wide(begin, size):
            cols = pl.ds(begin, size)
            part = (dot_tn(n0[...], d0[:, cols]) + dot_tn(n1[...], d1[:, cols])).astype(BF16)
            for h in range(size // 128):
                at = begin // 128 * rows + h * rows
                at = at if isinstance(at, int) else pl.multiple_of(at, rows)
                for f in range(count):
                    out_ref[f, pl.ds(at, rows), :] = part[
                        f * rows : (f + 1) * rows, h * 128 : (h + 1) * 128
                    ]

        def tall(c, carry):
            cols = pl.ds(pl.multiple_of(c * 256, 256), 256)
            part = dot_tn(h0[...], m0[:, cols]) + dot_tn(h1[...], m1[:, cols])
            for h in range(2):
                at = pl.multiple_of(base + (2 * c + h) * step, 16)
                for f in range(count):
                    value = part[f * hidden_rows : (f + 1) * hidden_rows, h * 128 : (h + 1) * 128]
                    if step > hidden_rows:
                        rest = jnp.zeros((step - hidden_rows, 128), F32)
                        value = jnp.concatenate([value, rest], axis=0)
                    out_ref[f, pl.ds(at, step), :] = value.astype(BF16)
            return carry

        def pair(c, carry):
            wide(pl.multiple_of(c * 256, 256), 256)
            return carry

        lax.fori_loop(0, both // 256, pair, 0)
        if both % 256:
            wide(both // 256 * 256, 128)
        lax.fori_loop(0, width // 256, tall, 0)

    arrays = [*normed, *d_acts, *hidden, *d_mlp]
    return pl.pallas_call(
        kernel,
        grid=(1,),
        in_specs=[pl.BlockSpec(a.shape, lambda i: (0, 0)) for a in arrays],
        out_specs=pl.BlockSpec((count, total, 128), lambda i: (0, 0, 0)),
        out_shape=jax.ShapeDtypeStruct((count, total, 128), BF16),
        cost_estimate=SMALL,
        name="hidden_terms",
    )(*arrays)


class Order:
    def __init__(self):
        self.last = None

    def tie(self, *values):
        if self.last is not None:
            values = lax.optimization_barrier(values + (self.last,))[:-1]
        return values if len(values) > 1 else values[0]

    def land(self, *values):
        values = lax.optimization_barrier(values + (self.last,))[:-1]
        self.last = values[0]
        return values if len(values) > 1 else values[0]

    def mark(self, value):
        self.last = value[0] if isinstance(value, (tuple, list)) else value
        return value

    def flip(self, array, bits):
        return lax.ppermute(self.tie(array), "seq", [(i, i ^ bits) for i in range(4)])

    def swap(self, pieces):
        return [self.flip(pieces[k], k) for k in (1, 2, 3)]


class Ring:
    def __init__(self, count, order):
        places = list(range(count))
        if count == 8:
            places = [0, 2, 4, 6, 7, 5, 3, 1]
        self.count = count
        self.order = order
        table = np.zeros((count, count), np.int32)
        for p, f in enumerate(places):
            table[f] = [places[(p + k) % count] for k in range(count)]
        self.slots = jnp.asarray(table)[lax.axis_index("fsdp")]
        nxt = [(places[i], places[(i + 1) % count]) for i in range(count)]
        self.perm = {1: nxt, -1: [(b, a) for a, b in nxt]}

    def send(self, array, way):
        return lax.ppermute(self.order.tie(array), "fsdp", self.perm[way])


def middle_row(rows):
    return (rows // 2 + 7) // 8 * 8


class Gather:
    def __init__(self, ring, own):
        self.ring, self.own, self.hop = ring, own, 0
        self.last = ring.count // 2
        self.ahead = self.behind = own
        self.pieces, self.places = [own], [(0, 0, own.shape[0])]

    def launch(self):
        self.hop += 1
        rows, half = self.own.shape[0], middle_row(self.own.shape[0])
        ahead, behind, t = self.ahead, self.behind, self.hop
        if t < self.last:
            self.places += [(self.ring.count - t, 0, rows), (t, 0, rows)]
        else:
            ahead, behind = ahead[:half], behind[half:]
            self.places += [(t, 0, half), (t, half, rows - half)]
        self.ahead, self.behind = self.ring.send(ahead, 1), self.ring.send(behind, -1)

    def land(self):
        self.ahead, self.behind = self.ring.order.land(self.ahead, self.behind)
        self.pieces += [self.ahead, self.behind]

    def rest(self):
        self.land()
        while self.hop < self.last - 1:
            self.launch()
            self.land()

    def collect(self, cuts=None):
        cuts = cuts or [(0, self.own.shape[0])]
        self.pieces[-1] = self.ring.order.tie(self.pieces[-1])
        return self.ring.order.mark(collect(self.pieces, self.ring.slots, self.places, cuts))


class Scatter:
    def __init__(self, ring, parts):
        self.ring, self.parts, self.hop = ring, parts, 0
        self.last = ring.count // 2
        self.came = None

    def kernel_call(self, offsets, body, came, outs, name):
        ring, parts = self.ring, self.parts
        count = ring.count

        def pick(part, offset):
            return pl.BlockSpec(
                (1,) + part.shape[1:], lambda i, slots: (slots[offset % count], 0, 0)
            )

        arrays, specs = [], []
        for part in parts:
            for offset in offsets:
                arrays.append(part)
                specs.append(pick(part, offset))
        for array in came:
            arrays.append(array)
            specs.append(pl.BlockSpec(array.shape, lambda i, slots: (0, 0)))
        return pl.pallas_call(
            lambda slots_ref, *refs: body(refs),
            grid_spec=pltpu.PrefetchScalarGridSpec(
                num_scalar_prefetch=1,
                grid=(1,),
                in_specs=specs,
                out_specs=[pl.BlockSpec(o, lambda i, slots: (0, 0)) for o in outs],
            ),
            out_shape=[jax.ShapeDtypeStruct(o, BF16) for o in outs],
            cost_estimate=SMALL,
            name=name,
        )(ring.slots, *arrays)

    def launch(self):
        self.hop += 1
        order, parts, n = self.ring.order, self.parts, len(self.parts)
        t = self.last + 1 - self.hop
        tops = [middle_row(p.shape[1]) for p in parts]
        if self.hop == 1:
            parts = order.tie(*parts)
            self.parts = parts = list(parts) if n > 1 else [parts]

            def first(refs):
                for p in range(n):
                    refs[n + 2 * p][...] = refs[p][0, : tops[p]]
                    refs[n + 2 * p + 1][...] = refs[p][0, tops[p] :]

            outs = []
            for p, part in enumerate(parts):
                outs += [(tops[p], part.shape[2]), (part.shape[1] - tops[p], part.shape[2])]
            send = self.kernel_call([t], first, [], outs, "scatter_first")
        else:

            def middle(refs):
                came, outs = refs[2 * n : 4 * n], refs[4 * n :]
                for p in range(n):
                    for way in range(2):
                        local, got = refs[2 * p + way], came[2 * p + way]
                        rows = slice(0, local.shape[1])
                        if self.hop == 2:
                            rows = slice(0, tops[p]) if way == 0 else slice(tops[p], rows.stop)
                            outs[2 * p + way][...] = local[0]
                        outs[2 * p + way][rows, :] = (
                            local[0, rows].astype(F32) + got[...].astype(F32)
                        ).astype(BF16)

            outs = []
            for part in parts:
                outs += [part.shape[1:]] * 2
            self.came[0] = order.tie(self.came[0])
            send = self.kernel_call([t, -t], middle, self.came, outs, "scatter_add")
        order.mark(send)
        self.came = [self.ring.send(array, 1 - 2 * (i % 2)) for i, array in enumerate(send)]

    def land(self):
        self.came = list(self.ring.order.land(*self.came))

    def rest(self):
        self.land()
        while self.hop < self.last:
            self.launch()
            self.land()

    def total(self):
        n = len(self.parts)

        def body(refs):
            for p in range(n):
                near = refs[n + 2 * p][...].astype(F32) + refs[n + 2 * p + 1][...].astype(F32)
                refs[3 * n + p][...] = (refs[p][0].astype(F32) + near).astype(BF16)

        outs = [part.shape[1:] for part in self.parts]
        self.came[0] = self.ring.order.tie(self.came[0])
        return self.ring.order.mark(self.kernel_call([0], body, self.came, outs, "scatter_sum"))


def per_device(
    latent,
    embed,
    seg_ids,
    positions,
    adapter_weight,
    query_weight,
    key_weight,
    value_weight,
    out_weight,
    gate_weight,
    up_weight,
    down_weight,
    gain_one,
    gain_two,
    gain_three,
    gain_four,
    cotangent,
):
    member = lax.axis_index("seq")
    count = lax.axis_size("fsdp")
    order = Order()
    ring = Ring(count, order)
    tokens, width = latent.shape[1], latent.shape[2]
    length = tokens * 4
    quarter = width // 4
    rows = query_weight.shape[0]
    adapter_rows = adapter_weight.shape[0]
    hidden_rows = down_weight.shape[0] // 4
    hidden_width = hidden_rows * count
    two = 2 * tokens

    def stack(*pieces):
        return jnp.concatenate(pieces, axis=0)

    def shares(part):
        return part.reshape(count, part.shape[0] // count, part.shape[1])

    def low(array):
        return array.astype(BF16)

    def high(array):
        return array.astype(F32)

    who = jnp.full((1,), member, jnp.int32)

    first_own, second_own = prepare(
        who,
        adapter_weight,
        (query_weight, key_weight, value_weight, out_weight),
        (gain_one, gain_two, gain_three, gain_four),
    )
    order.mark(first_own)
    joined = jnp.concatenate([latent[0], embed[0]], axis=1)
    order.mark(joined)
    adapters = Gather(ring, first_own)
    adapters.launch()
    across, beside = order.flip(joined, 2), order.flip(joined, 1)

    gate_up_own = order.mark(take_hidden(*order.tie(gate_weight, up_weight), who, count))
    down_own = lax.dynamic_slice_in_dim(
        order.tie(down_weight), member * hidden_rows, hidden_rows, 0
    )
    order.mark(down_own)
    qkvo = Gather(ring, second_own)
    gate_up, down = Gather(ring, gate_up_own), Gather(ring, down_own)

    def hop(*rings):
        for r in rings:
            r.land()
        for r in rings:
            r.launch()

    adapters.land()
    adapters.launch()
    hop(adapters)
    adapters.rest()
    adapters.launch()
    qkvo.launch()
    beside = order.land(beside)
    adapters.land()
    hop(qkvo)
    adapter_cols, gains = adapters.collect([(0, adapter_rows), (adapter_rows, adapter_rows + 8)])
    adapter_cols = adapter_cols.reshape(2 * width, quarter)
    gain_a, gain_b, gain_c, gain_d = [
        high(gains[:, g, :rows].reshape(1, width)) for g in range(4)
    ]
    stream_near = order.mark(stream_rows([order.tie(joined), beside], adapter_cols))
    across = order.land(across)
    diagonal = order.land(order.flip(across, 1))
    stream_far = order.mark(stream_rows([across, diagonal], adapter_cols))
    stream_cols = order.mark(stack(stream_near, stream_far))
    qkvo.land()
    stream_across, stream_beside = order.flip(stream_cols, 2), order.flip(stream_cols, 1)
    qkvo.launch()
    segments = order.tie(seg_ids)[0]
    starts = jnp.sum((segments[None, :] < segments[:, None]).astype(jnp.int32), axis=1)
    places = (jnp.arange(length, dtype=jnp.int32) - starts).astype(F32)
    info = jnp.concatenate([who, starts[::BLOCK] // BLOCK])
    lane = np.arange(128) % HD
    frequency = ROPE_BASE ** (-2.0 * jnp.asarray(lane % (HD // 2), F32) / HD)
    angles = places[:, None] * frequency[None, :]
    cosine = jnp.cos(angles)
    sine = jnp.sin(angles) * jnp.asarray(np.where(lane < HD // 2, -1.0, 1.0), F32)
    seg_row = segments.reshape(length // BLOCK, 1, BLOCK)
    seg_col = jnp.broadcast_to(segments[:, None], (length, 128))
    cosine, sine, seg_col, seg_row, info = order.land(cosine, sine, seg_col, seg_row, info)
    qkvo.rest()
    qkvo.launch()
    stream_beside, stream_across = order.land(stream_beside, stream_across)
    qkvo.land()
    stream_diagonal = order.flip(stream_across, 1)
    gate_up.launch()
    down.launch()
    qkvo_full = qkvo.collect()[0]
    stream_diagonal = order.land(stream_diagonal)

    out_sent = split_rows(order.tie(qkvo_full).reshape(width, width), who, 3 * quarter, width)
    order.mark(out_sent)
    out_came = order.swap(out_sent)
    normed_one, q_rows, k_rows, v_rows, stream = norm_qkv(
        [stream_cols, stream_beside, stream_across, stream_diagonal],
        gain_a,
        order.tie(qkvo_full),
        cosine,
        sine,
        who,
    )
    order.mark(q_rows)
    hop(gate_up, down)
    out_came = order.land(*out_came)
    out_rows = order.mark(assemble_cols([out_sent[0], *out_came], who, 1, BF16)[0])
    attended, lse = attend_forward(order.tie(q_rows), k_rows, v_rows, seg_row, seg_col, info)
    order.mark(attended)
    hop(gate_up, down)

    def weights_here():
        gate_up.land()
        down.land()
        wide, tall = gate_up.collect()[0], down.collect()[0]
        kept["hidden"] = wide.reshape(width, 2 * hidden_width), tall.reshape(hidden_width, width)

    kept = {}

    def scatter_seq(make, fill=None):
        far = order.mark(make(1))
        diagonal = order.land(order.flip(low(far[tokens:]), 1))
        crossing = order.mark(low(far[:tokens] + high(diagonal)))
        crossing = order.flip(crossing, 2)
        near = order.mark(make(0))
        beside = order.flip(low(near[tokens:]), 1)
        if fill is not None:
            fill()
        beside, crossing = order.land(beside, crossing)
        return near, beside, crossing

    branch = scatter_seq(
        lambda n: dot_nn(order.tie(attended)[n * two : (n + 1) * two], out_rows),
        lambda: hop(gate_up, down),
    )
    resid_one, middle, normed_own = rows_call(
        after_branch, branch, [stream], [gain_b, gain_c], ["wide", "wide", "low"], "after_branch"
    )(who)
    order.mark(normed_own)

    def gather_seq(own, fill=None, near=None):
        across, beside = order.flip(own, 2), order.flip(own, 1)
        beside = order.land(beside)
        close = order.mark(stack(own, beside))
        if fill is not None:
            fill()
        done = near(close) if near is not None else None
        across = order.land(across)
        diagonal = order.land(order.flip(across, 1))
        return close, order.mark(stack(across, diagonal)), done

    gate_act, up_act, hidden = [], [], []

    def into_hidden(rows_in):
        act = dot_nn(order.tie(rows_in), kept["hidden"][0])
        gate_act.append(act[:, :hidden_width])
        up_act.append(act[:, hidden_width:])
        hidden.append(low(gate_act[-1] / (1.0 + jnp.exp(-gate_act[-1])) * up_act[-1]))
        order.mark(hidden[-1])
        return order.mark(dot_nn(hidden[-1], kept["hidden"][1]))

    normed_near, normed_far, mlp_near = gather_seq(normed_own, weights_here, into_hidden)
    gate_up_full, down_full = kept["hidden"]
    mlp_far = into_hidden(normed_far)
    mlp = scatter_seq(lambda n: (mlp_near, mlp_far)[n])
    d_resid_two, d_mlp_own, result, gain_four_part = rows_call(
        after_mlp,
        mlp,
        [middle, cotangent[0]],
        [gain_d],
        ["wide", "low", "low", "sum"],
        "after_mlp",
    )(who)
    order.mark(d_mlp_own)

    def through_hidden(n, d_mlp):
        d_hidden = dot_nt(order.tie(d_mlp), down_full)
        gate, sigmoid = gate_act[n], 1.0 / (1.0 + jnp.exp(-gate_act[n]))
        d_gate = low(d_hidden * up_act[n] * sigmoid * (1.0 + gate * (1.0 - sigmoid)))
        d_up = low(d_hidden * (gate * sigmoid))
        return order.mark(jnp.concatenate([d_gate, d_up], axis=1))

    d_near, d_far, d_gate_up_near = gather_seq(
        d_mlp_own, None, lambda d_mlp: through_hidden(0, d_mlp)
    )
    d_gate_up = [d_gate_up_near, through_hidden(1, d_far)]
    rings = {}

    def hidden_grads():
        parts = hidden_terms(
            [order.tie(normed_near), normed_far], d_gate_up, hidden, [d_near, d_far], count
        )
        order.mark(parts)
        kept["hidden_sum"] = lax.psum_scatter(parts, "fsdp", scatter_dimension=0)

    d_normed_three = scatter_seq(
        lambda n: dot_nt(order.tie(d_gate_up[n]), gate_up_full), hidden_grads
    )
    d_resid_one, d_branch_own, gain_three_part, gain_two_part = rows_call(
        after_hidden,
        d_normed_three,
        [middle, resid_one, d_resid_two],
        [gain_b, gain_c],
        ["wide", "low", "sum", "sum"],
        "after_hidden",
    )(who)
    order.mark(d_branch_own)

    def into_attended(n, d_branch):
        grads = order.mark(low(dot_nt(order.tie(d_branch), out_rows)))
        return grads, order.mark(dot_tn(order.tie(attended)[n * two : (n + 1) * two], d_branch))

    _, d_branch_far, near_terms = gather_seq(
        d_branch_own, None, lambda d_branch: into_attended(0, d_branch)
    )
    adapter_across, adapter_beside = order.flip(adapter_cols, 2), order.flip(adapter_cols, 1)
    far_terms = into_attended(1, d_branch_far)
    d_attended = order.mark(stack(near_terms[0], far_terms[0]))
    out_part = order.mark(low(near_terms[1] + far_terms[1]))
    out_split = split_cols(order.tie(out_part), who)
    order.mark(out_split)
    out_sums = order.swap(out_split)
    d_qkv = attend_backward(
        q_rows,
        k_rows,
        v_rows,
        order.tie(d_attended),
        attended,
        lse,
        cosine,
        sine,
        seg_row,
        seg_col,
        info,
    )
    order.mark(d_qkv)
    qkv_cols = qkvo_full.reshape(width, width)[:, : 3 * quarter]

    def qkv_grads():
        sums = order.land(*out_sums)
        out_terms = assemble_rows([out_split[0], *sums], who, BF16)
        order.mark(out_terms)
        qkv_part = order.mark(low(dot_tn(order.tie(normed_one), d_qkv)))
        both = jnp.concatenate([shares(qkv_part), shares(out_terms)], axis=2)
        order.mark(both)
        kept["diagonal"] = order.flip(kept["across"], 1)
        rings["qkvo"] = Scatter(ring, [both])
        rings["qkvo"].launch()

    def into_normed(n):
        terms = dot_nt(order.tie(d_qkv)[n * two : (n + 1) * two], qkv_cols)
        if n == 1:
            order.mark(terms)
            kept["across"], kept["beside"] = order.land(adapter_across, adapter_beside)
            terms = order.tie(terms)
        return terms

    d_normed_one = scatter_seq(into_normed, qkv_grads)
    *d_split, gain_one_part = rows_call(
        after_attention,
        d_normed_one,
        [stream, d_resid_one],
        [gain_a],
        ["split"] * 4 + ["sum"],
        "after_attention",
    )(who)
    order.mark(d_split)
    d_cols = order.swap(d_split)
    hop(rings["qkvo"])
    d_cols = [d_split[0], *order.land(*d_cols)]
    hop(rings["qkvo"])
    adapter_part = adapter_terms(
        [order.tie(joined), beside, across, diagonal],
        d_cols,
        [gain_one_part, gain_two_part, gain_three_part, gain_four_part],
        count,
    )
    order.mark(adapter_part)
    rings["adapter"] = Scatter(ring, [adapter_part])
    rings["adapter"].launch()

    def exchange(total):
        return total, order.flip(total, 1), order.flip(total, 2)

    def settle(pieces):
        beside, across = order.land(*pieces[1:])
        return [pieces[0], beside, across, order.flip(across, 1)]

    hop(rings["qkvo"])
    kept["hidden_sum"] = order.land(kept["hidden_sum"])
    kept["hidden_grads"] = lax.all_gather(kept["hidden_sum"], "seq")
    adapter_diagonal = order.land(kept["diagonal"])
    latent_grad, embed_grad = joined_back(
        order.tie(d_split[0]),
        d_split[1:],
        [adapter_cols, kept["beside"], kept["across"], adapter_diagonal],
    )
    order.mark(latent_grad)
    hop(rings["adapter"])
    rings["qkvo"].rest()
    qkvo_done = exchange(rings["qkvo"].total()[0])
    hop(rings["adapter"])
    qkvo_done = settle(qkvo_done)
    hop(rings["adapter"])
    gate_grad, up_grad, down_grad = restore_hidden(
        order.land(kept["hidden_grads"]), rows, 2 * hidden_width, hidden_rows, width, count
    )
    order.mark(gate_grad)
    rings["adapter"].rest()
    last_done = exchange(rings["adapter"].total()[0])
    qkvo_done[3] = order.land(qkvo_done[3])
    query_grad, key_grad, value_grad, out_grad = assemble_cols(
        [order.tie(qkvo_done[0]), *qkvo_done[1:]], who, 4, F32
    )
    order.mark(query_grad)
    last_done = settle(last_done)
    last_done[3] = order.land(last_done[3])
    adapter_grad, *gain_grads = assemble_last(last_done, who, adapter_rows, rows)
    return (
        result[None],
        latent_grad[None],
        embed_grad[None],
        adapter_grad,
        query_grad,
        key_grad,
        value_grad,
        out_grad,
        gate_grad,
        up_grad,
        down_grad,
        gain_grads[0][0],
        gain_grads[1][0],
        gain_grads[2][0],
        gain_grads[3][0],
    )


def solution(mesh):
    rows, vector = P("fsdp", None), P("fsdp")
    tokens = P("fsdp", "seq", None)
    placed = (tokens, tokens, rows, P("fsdp", "seq")) + (rows,) * 8 + (vector,) * 4 + (tokens,)
    return jax.shard_map(
        per_device,
        mesh=mesh,
        in_specs=placed,
        out_specs=(tokens,) * 3 + (rows,) * 8 + (vector,) * 4,
        check_vma=False,
    )
```
